512 devices in a mesh: seq: 64 (over x, z), head: 8 (over y, core).
Axes of the slice: x: 4, y: 4, z: 16, core: 2. Of those that a mesh axis runs over, the one named last changes fastest.
Arguments:
- ssm_input: bfloat16 [16384, 8192], P('seq', 'head'), may hold values from -6 to 6
- bc_input: bfloat16 [16384, 2048], P('seq', 'head'), may hold values from -4 to 4
- conv_taps: float32 [4, 8192], P(None, 'head'), may hold values from -3 to 3
- conv_bias: float32 [8192], P('head'), may hold values from -1 to 0
- bc_taps: float32 [4, 2048], P(None, 'head'), may hold values from -3 to 3
- bc_bias: float32 [2048], P('head'), may hold values from -0.6 to 0.35
- step_input: float32 [128, 16384], P('head', 'seq'), may hold values from -4 to 4
- step_bias: float32 [128], P('head'), may hold values from -8 to -2
- decay_log: float32 [128], P('head'), may hold values from -8 to -1
- skip_gain: float32 [128], P('head'), may hold values from 0.5 to 2
- request_offset: int32 [16384], P('seq'), may hold values from 0 to 8191, as said below
Outputs:
- ssm_output: bfloat16 [16384, 8192], P('seq', 'head')
The draws below stay inside these ranges and needn't reach their ends.
Inputs may be any that keep to these rules, and one draw needn't show every extreme that they name: request_offset counts the earlier tokens of the token's request: 0 at the first token and wherever a request starts, else one more than at the token before; one request has exactly 8192 tokens and none has more.
All inputs are finite; a program needn't handle non-finite values.
Results may differ from the reference program's by a relative error of at most 0.0095.
Values may be sent and summed in bfloat16 or wider, within the bound.
A program may use at most 192 MiB of HBM per device.

```python
import jax
import jax.numpy as jnp
from jax import lax

HEADDIM = 64
STATE = 256
KERNEL = 4
BLOCK = 256
TOK_DEV = 256
TOKENS = 16384
HEADS = 128
GROUPS = 4
GROUP_HEADS = 32
CHANNELS = 8192


def head_rates(key):
    pick_key, spread_key, keep_key, rate_key = jax.random.split(jax.random.fold_in(key, 11), 4)
    slow_heads = jax.random.randint(pick_key, (HEADS,), 0, 10) < 5
    root_tokens = jnp.sqrt(jnp.float32(TOKENS))
    slow_step = jax.random.uniform(spread_key, (HEADS,), jnp.float32, 0.25, 0.6) / root_tokens
    kept_nats = jax.random.uniform(keep_key, (HEADS,), jnp.float32, 0.3, 1.5)
    slow_coef = kept_nats / (1.65 * slow_step * jnp.float32(TOKENS))
    lowest = jnp.log(jnp.float32(0.1) / jnp.float32(TOK_DEV))
    highest = jnp.log(jnp.float32(1.0 / 30.0))
    fraction = jax.random.uniform(rate_key, (HEADS,), jnp.float32, 0.0, 1.0)
    fast_rate = jnp.exp(lowest + (highest - lowest) * fraction)
    fast_coef = jnp.sqrt(fast_rate / 0.825)
    fast_step = 0.5 * fast_coef
    step_value = jnp.where(slow_heads, slow_step, fast_step)
    coef_value = jnp.where(slow_heads, slow_coef, fast_coef)
    return (jnp.log(step_value).astype(jnp.float32), jnp.log(coef_value).astype(jnp.float32))


def draw_step_bias(key, part):
    return head_rates(key)[0]


def draw_decay_log(key, part):
    return head_rates(key)[1]


def draw_request_offset(key, part):
    place_key, start_key = jax.random.split(jax.random.fold_in(key, 23))
    half_tokens = TOKENS // 2
    long_start = jax.random.randint(place_key, (), 0, half_tokens + 1)
    places = lax.iota(jnp.int32, TOKENS)
    starts = jax.random.randint(start_key, (TOKENS,), 0, 2 * TOK_DEV) == 0
    inside = (places > long_start) & (places < long_start + half_tokens)
    starts = jnp.where(inside, False, starts)
    starts = starts | (places == 0) | (places == long_start) | (places == long_start + half_tokens)
    latest = lax.cummax(jnp.where(starts, places, 0), axis=0)
    return (places - latest).astype(jnp.int32)


def steps_of(own_key, shape, cuts, least, largest):
    loudness, own = 1.0, jax.random.fold_in(own_key, 6)
    for dim, blocks in cuts:
        heights = jnp.exp(jax.random.uniform(jax.random.fold_in(own, dim), (blocks,), jnp.float32, least / len(cuts), largest / len(cuts)))
        loudness = loudness * jnp.repeat(heights, shape[dim] // blocks).reshape([-1 if axis == dim else 1 for axis in range(len(shape))])
    return loudness


def centred(own_key, shape, spread, most, shards=(), held_as=jnp.bfloat16):
    gain = steps_of(own_key, shape, shards, -0.22, 0.18) if shards else 1.0
    entries = jax.random.normal(own_key, shape, jnp.float32) * spread * gain
    return jnp.minimum(jnp.maximum(entries, -most), most).astype(held_as)


def setup_inputs(seed: int = 0) -> dict:
    arg_keys = jax.random.split(jax.random.key(seed), 12)
    ssm_input = centred(arg_keys[0], (TOKENS, CHANNELS), 1.0, 6.0, ((0, 64), (1, 8)))
    bc_input = centred(arg_keys[1], (TOKENS, GROUPS * 2 * STATE), 0.5, 4.0, ((0, 64), (1, 8)))
    conv_taps = centred(arg_keys[2], (KERNEL, CHANNELS), KERNEL ** -0.5, 3.0, ((1, 8),), jnp.float32)
    conv_bias = jnp.clip(-1.0 + 1.0 * jax.random.uniform(arg_keys[3], (CHANNELS,), jnp.float32) ** steps_of(arg_keys[3], (CHANNELS,), ((0, 8),), -0.2, 0.2), -1.0, 0.0)
    bc_taps = centred(arg_keys[4], (KERNEL, GROUPS * 2 * STATE), KERNEL ** -0.5, 3.0, ((1, 8),), jnp.float32)
    bc_bias = jnp.clip(-0.6 + 0.95000002 * jax.random.uniform(arg_keys[5], (GROUPS * 2 * STATE,), jnp.float32) ** steps_of(arg_keys[5], (GROUPS * 2 * STATE,), ((0, 8),), -0.2, 0.2), -0.6, 0.35)
    step_input = centred(arg_keys[6], (HEADS, TOKENS), 1.0, 4.0, ((0, 8), (1, 64)), jnp.float32)
    step_bias = draw_step_bias(jax.random.fold_in(arg_keys[11], 71), 0)
    decay_log = draw_decay_log(jax.random.fold_in(arg_keys[11], 71), 0)
    skip_gain = jnp.clip(0.5 + 1.5 * jax.random.uniform(arg_keys[9], (HEADS,), jnp.float32) ** steps_of(arg_keys[9], (HEADS,), ((0, 8),), -0.2, 0.2), 0.5, 2.0)
    request_offset = draw_request_offset(jax.random.fold_in(arg_keys[11], 71), 0)
    return {"ssm_input": ssm_input, "bc_input": bc_input, "conv_taps": conv_taps, "conv_bias": conv_bias, "bc_taps": bc_taps, "bc_bias": bc_bias, "step_input": step_input, "step_bias": step_bias, "decay_log": decay_log, "skip_gain": skip_gain, "request_offset": request_offset}


def conv_silu(source, tap_weights, tap_bias, offset):
    tok_rows = source.shape[0]
    tap_count = tap_weights.shape[0]
    summed = jnp.zeros(source.shape, jnp.float32) + tap_bias[None, :]
    for lag_steps in range(tap_count):
        shifted = jnp.pad(source, ((lag_steps, 0), (0, 0)))[:tok_rows].astype(jnp.float32)
        in_request = (offset >= lag_steps).astype(jnp.float32)[:, None]
        summed = summed + tap_weights[tap_count - 1 - lag_steps][None, :] * shifted * in_request
    return jax.nn.silu(summed).astype(jnp.bfloat16)


def reference(ssm_input, bc_input, conv_taps, conv_bias, bc_taps, bc_bias, step_input, step_bias, decay_log, skip_gain, request_offset):
    precise = lax.Precision.HIGHEST
    x_conv = conv_silu(ssm_input, conv_taps, conv_bias, request_offset)
    bc_conv = conv_silu(bc_input, bc_taps, bc_bias, request_offset)
    time_step = jax.nn.softplus(step_input + step_bias[:, None])
    log_decay = -jnp.exp(decay_log)[:, None] * time_step
    block_count = TOKENS // BLOCK
    blocked = (x_conv.reshape(block_count, BLOCK, HEADS, HEADDIM),
               bc_conv.reshape(block_count, BLOCK, GROUPS, 2, STATE),
               time_step.reshape(HEADS, block_count, BLOCK).transpose(1, 0, 2),
               log_decay.reshape(HEADS, block_count, BLOCK).transpose(1, 0, 2),
               request_offset.reshape(block_count, BLOCK))

    def advance(entering, block_item):
        x_block, bc_block, step_block, decay_block, offset_block = block_item
        b_group = bc_block[:, :, 0, :].astype(jnp.float32)
        c_group = bc_block[:, :, 1, :].astype(jnp.float32)
        b_head = jnp.repeat(b_group, GROUP_HEADS, axis=1)
        c_head = jnp.repeat(c_group, GROUP_HEADS, axis=1)
        x_float = x_block.astype(jnp.float32)
        rate_sum = jnp.cumsum(decay_block, axis=1)
        positions = lax.iota(jnp.int32, BLOCK)
        linked = (positions[None, :] <= positions[:, None]) & (offset_block[:, None] >= positions[:, None] - positions[None, :])
        scores = jnp.einsum('ign,jgn->gij', c_group, b_group, precision=precise)
        scores = jnp.repeat(scores, GROUP_HEADS, axis=0)
        rate_gap = jnp.where(linked[None], rate_sum[:, :, None] - rate_sum[:, None, :], -1e30)
        weights = (scores * jnp.exp(rate_gap) * step_block[:, None, :]).astype(jnp.bfloat16)
        intra_part = jnp.einsum('hij,jhp->ihp', weights.astype(jnp.float32), x_float, precision=precise)
        tail_gap = jnp.where(offset_block[-1] >= BLOCK - 1 - positions[None, :], rate_sum[:, -1:] - rate_sum, -1e30)
        weighted_b = (b_head.transpose(1, 0, 2) * (jnp.exp(tail_gap) * step_block)[:, :, None]).astype(jnp.bfloat16)
        block_state = jnp.einsum('hjn,jhp->hnp', weighted_b.astype(jnp.float32), x_float, precision=precise)
        carry_scale = jnp.exp(rate_sum) * (offset_block >= positions + 1).astype(jnp.float32)[None, :]
        inter_part = jnp.einsum('ihn,hnp->ihp', c_head, entering, precision=precise) * carry_scale.T[:, :, None]
        passing = jnp.exp(rate_sum[:, -1]) * (offset_block[-1] >= BLOCK).astype(jnp.float32)
        block_out = intra_part + inter_part + skip_gain[None, :, None] * x_float
        next_state = passing[:, None, None] * entering + block_state
        return next_state, block_out.reshape(BLOCK, HEADS * HEADDIM).astype(jnp.bfloat16)

    start_state = jnp.zeros((HEADS, STATE, HEADDIM), jnp.float32)
    final_state, outputs = lax.scan(advance, start_state, blocked)
    return outputs.reshape(TOKENS, HEADS * HEADDIM)
```

```python
import functools

import jax
import jax.numpy as jnp
from jax import lax
from jax.experimental import pallas as pl
from jax.experimental.pallas import tpu as pltpu
from jax.sharding import PartitionSpec as P

HEADDIM = 64
LANES = 128
MESH = pl.DeviceIdType.MESH
F32 = jnp.float32
BF16 = jnp.bfloat16


def split3(value):
    high = value.astype(BF16)
    rest = value - high.astype(F32)
    mid = rest.astype(BF16)
    low = (rest - mid.astype(F32)).astype(BF16)
    return high, mid, low


def iota(shape, axis):
    return lax.broadcasted_iota(jnp.int32, shape, axis)


def silu(v):
    return v / (1.0 + jnp.exp(-v))


def kernel(
    nx, nz, nc,
    xin, bcin, taps, bias, bct, bcb, step, sbias, dlog, sgain, off,
    out,
    xf, xfb, xc, offb, sexp, rexp, rate, td, xhalo, bchalo, bown, bother, bsel, csel,
    smask, y, st, recv, eb, ent, pas_s, pas_r, pexp, tb, tr, ptot, ptr,
    fs, fr, rs, rr, ts, tsr, ps, pr, as_, ar, hs, hr,
):
    tok = xin.shape[0]
    chans = xin.shape[1]
    state = bcin.shape[1]
    heads = step.shape[0]
    width = chans // nc
    rows = state // nz
    s = lax.axis_index("seq")
    head = lax.axis_index("head")
    x = s // nz
    z = lax.rem(s, nz)
    count = nx * nz
    nxt = lax.rem(s + 1, count)
    prv = lax.rem(s + count - 1, count)
    partner = head + 1 - 2 * lax.rem(head, 2)

    barrier = pltpu.get_barrier_semaphore()

    def greet(seq_index, head_index):
        pl.semaphore_signal(barrier, inc=1, device_id=(seq_index, head_index), device_id_type=MESH)

    greet(nxt, head)
    greet(prv, head)
    greet(s, partner)

    @pl.loop(1, nz)
    def _(d):
        greet(x * nz + lax.rem(z + d, nz), head)

    @pl.loop(1, nx)
    def _(d):
        greet(lax.rem(x + d, nx) * nz + z, head)

    off_row = jnp.minimum(off[...], tok).astype(F32)
    eye = (iota((tok, tok), 0) == iota((tok, tok), 1)).astype(BF16)
    off_rows = jnp.broadcast_to(off_row, (LANES, tok)).astype(BF16)
    offb[...] = lax.dot_general(eye, off_rows, (((1,), (1,)), ((), ())), preferred_element_type=F32)
    off_last = off_row[:, tok - 1 : tok]

    eye_h = iota((heads, heads), 0) == iota((heads, heads), 1)

    def column(row):
        return jnp.sum(jnp.where(eye_h, jnp.broadcast_to(row, (heads, heads)), 0.0), axis=1, keepdims=True)

    time_step = jnp.log1p(jnp.exp(step[...] + column(sbias[...])))
    log_decay = -jnp.exp(column(dlog[...])) * time_step
    upper = (iota((tok, tok), 0) <= iota((tok, tok), 1)).astype(F32)
    rate_row = jnp.dot(log_decay, upper, precision=lax.Precision.HIGHEST, preferred_element_type=F32)
    rate[...] = rate_row
    td[...] = time_step
    rate_last = rate_row[:, tok - 1 : tok]
    position = iota((1, tok), 1).astype(F32)
    tail = off_last >= (tok - 1) - position
    s_row = jnp.where(tail, jnp.exp(rate_last - rate_row), 0.0) * time_step
    passing = jnp.where(off_last >= tok, jnp.exp(rate_last), 0.0)

    spread = (lax.rem(iota((3 * heads, chans), 0), heads) == iota((3 * heads, chans), 1) // HEADDIM).astype(BF16)

    def expand(value):
        return lax.dot_general(
            jnp.concatenate(split3(value), axis=0), spread, (((0,), (0,)), ((), ())), preferred_element_type=F32
        )

    sexp[...] = expand(s_row)
    rexp[...] = expand(rate_row)

    def as_row(col):
        return jnp.sum(
            jnp.where(iota((heads, LANES), 0) == iota((heads, LANES), 1), jnp.broadcast_to(col, (heads, LANES)), 0.0),
            axis=0,
            keepdims=True,
        )

    pas_s[...] = jnp.broadcast_to(as_row(passing), (8, LANES))
    pas_r[pl.ds(z, 1)] = pas_s[...][None]

    def halo_copy(which):
        src = (xin, bcin)[which].at[pl.ds(tok - 16, 16), :]
        dst = (xhalo, bchalo)[which]
        return pltpu.make_async_remote_copy(
            src, dst, hs.at[which], hr.at[which], device_id=(nxt, head), device_id_type=MESH
        )

    def partner_copy():
        return pltpu.make_async_remote_copy(
            bown, bother, hs.at[2], hr.at[2], device_id=(s, partner), device_id_type=MESH
        )

    def pas_copy(d):
        to = x * nz + lax.rem(z + d, nz)
        return pltpu.make_async_remote_copy(
            pas_s, pas_r.at[z], as_.at[d], ar.at[d], device_id=(to, head), device_id_type=MESH
        )

    def fwd_copy(c, d):
        to = lax.rem(z + d, nz)
        return pltpu.make_async_remote_copy(
            st.at[c, to], recv.at[c, z], fs.at[c, d], fr.at[c, d], device_id=(x * nz + to, head), device_id_type=MESH
        )

    def ret_copy(c, d):
        to = lax.rem(z + d, nz)
        return pltpu.make_async_remote_copy(
            eb.at[c, to], ent.at[c, z], rs.at[c, d], rr.at[c, d], device_id=(x * nz + to, head), device_id_type=MESH
        )

    def total_copy(c, d):
        to = lax.rem(x + d, nx) * nz + z
        return pltpu.make_async_remote_copy(
            tb.at[c], tr.at[c, x], ts.at[c, d], tsr.at[c, d], device_id=(to, head), device_id_type=MESH
        )

    def ptot_copy(d):
        to = lax.rem(x + d, nx) * nz + z
        return pltpu.make_async_remote_copy(
            ptot, ptr.at[x], ps.at[d], pr.at[d], device_id=(to, head), device_id_type=MESH
        )

    pl.semaphore_wait(barrier, (nz - 1) + (nx - 1) + 3)
    halo_copy(1).start()
    halo_copy(0).start()

    @pl.loop(1, nz)
    def _(d):
        pas_copy(d).start()

    @pl.loop(0, chans // LANES)
    def _(i):
        cols = pl.ds(pl.multiple_of(i * LANES, LANES), LANES)
        xf[pl.ds(8, tok), cols] = xin[:, cols].astype(F32)
        acc = jnp.broadcast_to(bias[:, cols], (tok, LANES))
        for lag in range(4):
            term = taps[3 - lag : 4 - lag, cols] * xf[pl.ds(8 - lag, tok), cols]
            acc = acc + (term if lag == 0 else jnp.where(offb[...] >= lag, term, 0.0))
        xc[:, cols] = silu(acc).astype(BF16)

    xfb[pl.ds(8, tok), :] = bcin[...].astype(F32)
    halo_copy(1).wait()
    xfb[pl.ds(0, 8), :] = bchalo[...].astype(F32)[8:16]
    for i in range(state // LANES):
        cols = slice(i * LANES, (i + 1) * LANES)
        acc = jnp.broadcast_to(bcb[:, cols], (tok, LANES))
        for lag in range(4):
            term = bct[3 - lag : 4 - lag, cols] * xfb[pl.ds(8 - lag, tok), cols]
            acc = acc + (term if lag == 0 else jnp.where(offb[...] >= lag, term, 0.0))
        bown[:, cols] = silu(acc).astype(BF16)
    partner_copy().start()

    halo_copy(0).wait()
    xf[pl.ds(0, 8), :] = xhalo[...].astype(F32)[8:16]
    acc = jnp.broadcast_to(bias[...], (16, chans))
    off_top = offb[0:16, 0:1]
    for lag in range(4):
        term = taps[3 - lag : 4 - lag, :] * xf[pl.ds(8 - lag, 16), :]
        acc = acc + (term if lag == 0 else jnp.where(off_top >= lag, term, 0.0))
    xc[0:16, :] = silu(acc).astype(BF16)

    partner_copy().wait()
    even = lax.rem(head, 2) == 0
    bsel[...] = jnp.where(even, bown[...], bother[...])
    csel[...] = jnp.where(even, bother[...], bown[...])

    for c in range(nc):
        cols = slice(c * width, (c + 1) * width)
        scaled = (xc[:, cols].astype(F32) * sexp[:, cols]).astype(BF16)
        block_state = lax.dot_general(bsel[...], scaled, (((0,), (0,)), ((), ())), preferred_element_type=F32)
        st[c] = block_state.astype(BF16).reshape(nz, rows, width)
        recv[c, pl.ds(z, 1)] = st[c, pl.ds(z, 1)]

        @pl.loop(1, nz)
        def _(d):
            fwd_copy(c, d).start()

    scores = lax.dot_general(csel[...], bsel[...], (((1,), (1,)), ((), ())), preferred_element_type=F32)
    row_i, col_j = iota((tok, tok), 0).astype(F32), iota((tok, tok), 1).astype(F32)
    linked = (col_j <= row_i) & (offb[:, 0:1] >= row_i - col_j)
    smask[...] = jnp.where(linked, scores, 0.0)
    spread_f = iota((heads, chans), 0) == iota((heads, chans), 1) // HEADDIM
    skip = jnp.sum(jnp.where(spread_f, jnp.broadcast_to(column(sgain[...]), (heads, chans)), 0.0), axis=0, keepdims=True)
    y[...] = skip * xc[...].astype(F32)
    first = iota((tok, LANES), 1) < HEADDIM

    @pl.loop(0, heads // 2)
    def _(p):
        cols = pl.ds(pl.multiple_of(p * LANES, LANES), LANES)
        rate_cols = rexp[:, cols]
        xp = xc[:, cols]
        parts = []
        for k in range(2):
            gap = jnp.minimum(rate_cols[:, k * HEADDIM : k * HEADDIM + 1] - rate[pl.ds(2 * p + k, 1), :], 0.0)
            weights = (smask[...] * jnp.exp(gap) * td[pl.ds(2 * p + k, 1), :]).astype(BF16)
            parts.append(jnp.dot(weights, xp, preferred_element_type=F32))
        y[:, cols] = y[:, cols] + jnp.where(first, parts[0], parts[1])

    @pl.loop(1, nz)
    def _(d):
        pas_copy(d).wait()

    spread_l = (iota((LANES, chans), 0) == iota((LANES, chans), 1) // HEADDIM).astype(BF16)

    def expand_rows(value):
        return sum(jnp.dot(part, spread_l, preferred_element_type=F32) for part in split3(value))

    pas_all = pas_r[:, 0, :]
    pexp[...] = expand_rows(pas_all)
    product = pas_all[0:1]
    for k in range(1, nz):
        product = product * pas_all[k : k + 1]
    ptot[...] = jnp.broadcast_to(product, (8, LANES))

    @pl.loop(1, nx)
    def _(d):
        ptot_copy(d).start()

    def advance(c, k, carried):
        cols = slice(c * width, (c + 1) * width)
        return pexp[pl.ds(k, 1), cols] * carried + recv[c, k].astype(F32)

    def totals(c):
        @pl.loop(1, nz)
        def _(d):
            fwd_copy(c, d).wait()

        total = lax.fori_loop(0, nz, lambda k, e: advance(c, k, e), jnp.zeros((rows, width), F32))
        tb[c] = total.astype(BF16)

        @pl.loop(1, nx)
        def _(d):
            total_copy(c, d).start()

    def give_back(c):
        if c == 0:

            @pl.loop(1, nx)
            def _(d):
                ptot_copy(d).wait()

        @pl.loop(1, nx)
        def _(d):
            total_copy(c, d).wait()

        cols = slice(c * width, (c + 1) * width)
        carried = jnp.zeros((rows, width), F32)
        for k in range(nx - 1):
            decay = expand_rows(ptr[k])[0:1, cols]
            longer = decay * carried + tr[c, k].astype(F32)
            carried = jnp.where(k < x, longer, carried)

        def pass_on(k, e):
            eb[c, k] = e.astype(BF16)
            return advance(c, k, e)

        lax.fori_loop(0, nz, pass_on, carried)
        ent[c, pl.ds(z, 1)] = eb[c, pl.ds(z, 1)]

        @pl.loop(1, nz)
        def _(d):
            ret_copy(c, d).start()

    def finish(c):
        @pl.loop(1, nz)
        def _(d):
            ret_copy(c, d).wait()

        cols = slice(c * width, (c + 1) * width)
        read = jnp.dot(csel[...], ent[c].reshape(state, width), preferred_element_type=F32)
        carries = offb[:, 0:1] >= iota((tok, 1), 0).astype(F32) + 1.0
        scale = jnp.where(carries, jnp.exp(rexp[:, cols]), 0.0)
        out[:, cols] = (y[:, cols] + read * scale).astype(BF16)

    for c in range(nc):
        totals(c)
        if c:
            give_back(c - 1)
    give_back(nc - 1)
    for c in range(nc):
        finish(c)


def on_device(nx, nz, nc, *args):
    (ssm_input, bc_input, conv_taps, conv_bias, bc_taps, bc_bias, step_input, step_bias, decay_log, skip_gain,
     request_offset) = args
    tok, chans = ssm_input.shape
    state = bc_input.shape[1]
    heads = step_input.shape[0]
    width, rows = chans // nc, state // nz
    vmem = pl.BlockSpec(memory_space=pltpu.VMEM)
    dma = pltpu.SemaphoreType.DMA
    scratch = [
        pltpu.VMEM((tok + 8, chans), F32),
        pltpu.VMEM((tok + 8, state), F32),
        pltpu.VMEM((tok, chans), BF16),
        pltpu.VMEM((tok, LANES), F32),
        pltpu.VMEM((tok, chans), F32),
        pltpu.VMEM((tok, chans), F32),
        pltpu.VMEM((heads, tok), F32),
        pltpu.VMEM((heads, tok), F32),
        pltpu.VMEM((16, chans), BF16),
        pltpu.VMEM((16, state), BF16),
        pltpu.VMEM((tok, state), BF16),
        pltpu.VMEM((tok, state), BF16),
        pltpu.VMEM((tok, state), BF16),
        pltpu.VMEM((tok, state), BF16),
        pltpu.VMEM((tok, tok), F32),
        pltpu.VMEM((tok, chans), F32),
        pltpu.VMEM((nc, nz, rows, width), BF16),
        pltpu.VMEM((nc, nz, rows, width), BF16),
        pltpu.VMEM((nc, nz, rows, width), BF16),
        pltpu.VMEM((nc, nz, rows, width), BF16),
        pltpu.VMEM((8, LANES), F32),
        pltpu.VMEM((nz, 8, LANES), F32),
        pltpu.VMEM((nz, chans), F32),
        pltpu.VMEM((nc, rows, width), BF16),
        pltpu.VMEM((nc, nx, rows, width), BF16),
        pltpu.VMEM((8, LANES), F32),
        pltpu.VMEM((nx, 8, LANES), F32),
        dma((nc, nz)), dma((nc, nz)), dma((nc, nz)), dma((nc, nz)),
        dma((nc, nx)), dma((nc, nx)), dma((nx,)), dma((nx,)), dma((nz,)), dma((nz,)), dma((3,)), dma((3,)),
    ]
    return pl.pallas_call(
        functools.partial(kernel, nx, nz, nc),
        out_shape=jax.ShapeDtypeStruct((tok, chans), BF16),
        in_specs=[vmem] * 11,
        out_specs=vmem,
        scratch_shapes=scratch,
        compiler_params=pltpu.CompilerParams(
            collective_id=0, has_side_effects=True, vmem_limit_bytes=40 << 20
        ),
    )(
        ssm_input, bc_input, conv_taps, conv_bias[None], bc_taps, bc_bias[None], step_input, step_bias[None],
        decay_log[None], skip_gain[None], request_offset[None],
    )


def solution(mesh, nx=4, nc=2):
    nz = mesh.shape["seq"] // nx
    return jax.shard_map(
        functools.partial(on_device, nx, nz, nc),
        mesh=mesh,
        in_specs=(
            P("seq", "head"),
            P("seq", "head"),
            P(None, "head"),
            P("head"),
            P(None, "head"),
            P("head"),
            P("head", "seq"),
            P("head"),
            P("head"),
            P("head"),
            P("seq"),
        ),
        out_specs=P("seq", "head"),
        check_vma=False,
    )
```

```python
import functools

import jax
import jax.numpy as jnp
from jax import lax
from jax.experimental import pallas as pl
from jax.experimental.pallas import tpu as pltpu
from jax.sharding import PartitionSpec as P

HEADDIM = 64
LANES = 128
MESH = pl.DeviceIdType.MESH
F32 = jnp.float32
BF16 = jnp.bfloat16


def split3(value):
    high = value.astype(BF16)
    rest = value - high.astype(F32)
    mid = rest.astype(BF16)
    low = (rest - mid.astype(F32)).astype(BF16)
    return high, mid, low


def iota(shape, axis):
    return lax.broadcasted_iota(jnp.int32, shape, axis)


def silu(v):
    return v / (1.0 + jnp.exp(-v))


def kernel(
    nx, ni, nr, nc,
    xin, bcin_h, taps_h, bias_h, bct_h, bcb_h, step_h, sbias_h, dlog_h, sgain_h, off_h,
    out,
    xv, bcin, taps, bias, bct, bcb, step, sbias, dlog, sgain, off,
    xf, xfb, xc, offb, sexp, xs, rexp, rate, td, skip, xhalo, bchalo, bown, bother, bsel, csel,
    smask, y, st, ra, gs, rb, kb, kr, eb, ent, pas_s, pas_r, gpas_s, gpas_r, pexp, gexp,
    ins, a_s, a_r, b_s, b_r, k_s, k_r, e_s, e_r, q_s, q_r, p_s, p_r, h_s, h_r, round_sem,
):
    tok, chans = xv.shape
    state = bcin.shape[1]
    heads = step.shape[0]
    width = chans // nc
    count = lax.axis_size("seq")
    nq = count // ni
    nb = nq // nr
    ng = nq // nx
    rows_a, rows_b, part_width = state // ni, state // ni // nr, width // nb
    s = lax.axis_index("seq")
    head = lax.axis_index("head")
    odd = lax.rem(head, 2)
    partner = head + 1 - 2 * odd
    nxt = lax.rem(s + 1, count)
    prv = lax.rem(s + count - 1, count)
    shift = odd * (ni // 2)
    place = lax.rem(s + shift, count)
    q, i = place // ni, lax.rem(place, ni)

    def device(q_at, i_at):
        return (lax.rem(q_at * ni + i_at + count - shift, count), head)

    def member(d):
        return lax.rem(i + d, ni)

    def group(d):
        return lax.rem(q + d, nq)

    loads = [
        pltpu.make_async_copy(src, dst, ins.at[k])
        for k, (src, dst) in enumerate(
            (
                (off_h, off), (step_h, step), (sbias_h, sbias), (dlog_h, dlog), (bcin_h, bcin), (xin, xv),
                (taps_h, taps), (bias_h, bias), (bct_h, bct), (bcb_h, bcb), (sgain_h, sgain),
            )
        )
    ]
    for load in loads:
        load.start()

    barrier = pltpu.get_barrier_semaphore()

    def greet(device_id):
        pl.semaphore_signal(barrier, inc=1, device_id=device_id, device_id_type=MESH)

    def beside(d):
        return device(q // ng * ng + lax.rem(lax.rem(q, ng) + d, ng), i)

    greet(beside(1))
    greet(beside(ng - 1))

    @pl.loop(1, ni)
    def _(d):
        greet(device(q, member(d)))

    @pl.loop(1, nx)
    def _(d):
        greet(device(group(d * ng), i))

    greet((nxt, head))
    greet((prv, head))
    greet((s, partner))

    def tell(r):
        for d in (1, ng - 1):
            pl.semaphore_signal(round_sem.at[r], inc=1, device_id=beside(d), device_id_type=MESH)

    def remote(src, dst, send, recv, device_id):
        return pltpu.make_async_remote_copy(src, dst, send, recv, device_id=device_id, device_id_type=MESH)

    def halo_copy(which):
        src = (xin, bcin_h)[which].at[pl.ds(tok - 16, 16), :]
        return remote(src, (xhalo, bchalo)[which], h_s.at[which], h_r.at[which], (nxt, head))

    def partner_copy():
        return remote(bown, bother, h_s.at[2], h_r.at[2], (s, partner))

    def pas_copy(d):
        return remote(pas_s, pas_r.at[i], q_s.at[d], q_r.at[d], device(q, member(d)))

    def gpas_copy(d):
        return remote(gpas_s, gpas_r.at[q], p_s.at[d], p_r.at[d], device(group(d), i))

    def a_copy(c, d):
        to = member(d)
        return remote(st.at[c, to], ra.at[c, i], a_s.at[c, d], a_r.at[c, d], device(q, to))

    def b_copy(c, d):
        to = group(d)
        return remote(gs.at[c, to], rb.at[c, q], b_s.at[c, d], b_r.at[c, d], device(to, i))

    def k_copy(c, d):
        to = group(d)
        return remote(kb.at[c, to], kr.at[c, q], k_s.at[c, d], k_r.at[c, d], device(to, i))

    def e_copy(c, d):
        to = member(d)
        return remote(eb.at[c, to], ent.at[c, i], e_s.at[c, d], e_r.at[c, d], device(q, to))

    def start(copy, n, *lead):
        @pl.loop(1, n)
        def _(d):
            copy(*lead, d).start()

    def wait(copy, n, *lead):
        @pl.loop(1, n)
        def _(d):
            copy(*lead, d).wait()

    for load in loads[:4]:
        load.wait()
    off_row = jnp.minimum(off[...], tok).astype(F32)
    eye = (iota((tok, tok), 0) == iota((tok, tok), 1)).astype(BF16)
    off_rows = jnp.broadcast_to(off_row, (LANES, tok)).astype(BF16)
    offb[...] = lax.dot_general(eye, off_rows, (((1,), (1,)), ((), ())), preferred_element_type=F32)
    off_last = off_row[:, tok - 1 : tok]

    eye_h = iota((heads, heads), 0) == iota((heads, heads), 1)

    def column(row):
        return jnp.sum(jnp.where(eye_h, jnp.broadcast_to(row, (heads, heads)), 0.0), axis=1, keepdims=True)

    time_step = jnp.log1p(jnp.exp(step[...] + column(sbias[...])))
    log_decay = -jnp.exp(column(dlog[...])) * time_step
    upper = (iota((tok, tok), 0) <= iota((tok, tok), 1)).astype(F32)
    rate_row = jnp.dot(log_decay, upper, precision=lax.Precision.HIGHEST, preferred_element_type=F32)
    rate[...] = rate_row
    td[...] = time_step
    rate_last = rate_row[:, tok - 1 : tok]
    position = iota((1, tok), 1).astype(F32)
    tail = off_last >= (tok - 1) - position
    s_row = jnp.where(tail, jnp.exp(rate_last - rate_row), 0.0) * time_step
    passing = jnp.where(off_last >= tok, jnp.exp(rate_last), 0.0)

    pick = iota((heads, LANES), 0) == iota((heads, LANES), 1)
    as_row = jnp.sum(jnp.where(pick, jnp.broadcast_to(passing, (heads, LANES)), 0.0), axis=0, keepdims=True)
    pas_s[...] = jnp.broadcast_to(as_row, (8, LANES))

    spread = (lax.rem(iota((3 * heads, chans), 0), heads) == iota((3 * heads, chans), 1) // HEADDIM).astype(BF16)

    def expand(value):
        return lax.dot_general(
            jnp.concatenate(split3(value), axis=0), spread, (((0,), (0,)), ((), ())), preferred_element_type=F32
        )

    sexp[...] = expand(s_row)
    rexp[...] = expand(rate_row)

    for load in loads[5:8]:
        load.wait()

    @pl.loop(0, chans // LANES)
    def _(n):
        cols = pl.ds(pl.multiple_of(n * LANES, LANES), LANES)
        xf[pl.ds(8, tok), cols] = xv[:, cols].astype(F32)
        acc = jnp.broadcast_to(bias[:, cols], (tok, LANES))
        for lag in range(4):
            term = taps[3 - lag : 4 - lag, cols] * xf[pl.ds(8 - lag, tok), cols]
            acc = acc + (term if lag == 0 else jnp.where(offb[...] >= lag, term, 0.0))
        xc[:, cols] = silu(acc).astype(BF16)

    pl.semaphore_wait(barrier, (ni - 1) + (nx - 1) + 5)
    halo_copy(1).start()
    halo_copy(0).start()
    tell(0)
    pas_r[pl.ds(i, 1)] = pas_s[...][None]
    start(pas_copy, ni)

    @pl.loop(0, chans // LANES)
    def _(n):
        cols = pl.ds(pl.multiple_of(n * LANES, LANES), LANES)
        xs[:, cols] = (xc[:, cols].astype(F32) * sexp[:, cols]).astype(BF16)

    loads[4].wait()
    loads[8].wait()
    loads[9].wait()
    xfb[pl.ds(8, tok), :] = bcin[...].astype(F32)
    halo_copy(1).wait()
    xfb[pl.ds(0, 8), :] = bchalo[...].astype(F32)[8:16]
    for n in range(state // LANES):
        cols = slice(n * LANES, (n + 1) * LANES)
        acc = jnp.broadcast_to(bcb[:, cols], (tok, LANES))
        for lag in range(4):
            term = bct[3 - lag : 4 - lag, cols] * xfb[pl.ds(8 - lag, tok), cols]
            acc = acc + (term if lag == 0 else jnp.where(offb[...] >= lag, term, 0.0))
        bown[:, cols] = silu(acc).astype(BF16)
    partner_copy().start()

    halo_copy(0).wait()
    xf[pl.ds(0, 8), :] = xhalo[...].astype(F32)[8:16]
    acc = jnp.broadcast_to(bias[...], (16, chans))
    off_top = offb[0:16, 0:1]
    for lag in range(4):
        term = taps[3 - lag : 4 - lag, :] * xf[pl.ds(8 - lag, 16), :]
        acc = acc + (term if lag == 0 else jnp.where(off_top >= lag, term, 0.0))
    top = silu(acc).astype(BF16)
    xc[0:16, :] = top
    xs[0:16, :] = (top.astype(F32) * sexp[0:16, :]).astype(BF16)

    partner_copy().wait()
    even = odd == 0
    bsel[...] = jnp.where(even, bown[...], bother[...])
    csel[...] = jnp.where(even, bother[...], bown[...])

    for c in range(nc):
        cols = slice(c * width, (c + 1) * width)
        block_state = lax.dot_general(bsel[...], xs[:, cols], (((0,), (0,)), ((), ())), preferred_element_type=F32)
        st[c] = block_state.astype(BF16).reshape(ni, rows_a, width)
        start(a_copy, ni, c)
        ra[c, pl.ds(i, 1)] = st[c, pl.ds(i, 1)]

    pl.semaphore_wait(round_sem.at[0], 2)
    tell(1)

    wait(pas_copy, ni)
    pas_all = pas_r[:, 0, :]
    product = pas_all[0:1]
    for m in range(1, ni):
        product = product * pas_all[m : m + 1]
    gpas_s[...] = jnp.broadcast_to(product, (8, LANES))
    gpas_r[pl.ds(q, 1)] = gpas_s[...][None]

    spread_l = (iota((LANES, chans), 0) == iota((LANES, chans), 1) // HEADDIM).astype(BF16)

    def expand_rows(value):
        return sum(jnp.dot(part, spread_l, preferred_element_type=F32) for part in split3(value))

    pexp[...] = expand_rows(pas_all)

    loads[10].wait()
    scores = lax.dot_general(csel[...], bsel[...], (((1,), (1,)), ((), ())), preferred_element_type=F32)
    row_i, col_j = iota((tok, tok), 0).astype(F32), iota((tok, tok), 1).astype(F32)
    linked = (col_j <= row_i) & (offb[:, 0:1] >= row_i - col_j)
    smask[...] = jnp.where(linked, scores, 0.0)
    spread_f = iota((heads, chans), 0) == iota((heads, chans), 1) // HEADDIM
    skip[...] = jnp.sum(jnp.where(spread_f, jnp.broadcast_to(column(sgain[...]), (heads, chans)), 0.0), axis=0, keepdims=True)
    first = iota((tok, LANES), 1) < HEADDIM
    carries = offb[...] >= iota((tok, LANES), 0).astype(F32) + 1.0

    @pl.loop(0, heads // 2)
    def _(p):
        cols = pl.ds(pl.multiple_of(p * LANES, LANES), LANES)
        rate_cols = rexp[:, cols]
        xp = xc[:, cols]
        parts = []
        for k in range(2):
            gap = jnp.minimum(rate_cols[:, k * HEADDIM : k * HEADDIM + 1] - rate[pl.ds(2 * p + k, 1), :], 0.0)
            weights = (smask[...] * jnp.exp(gap) * td[pl.ds(2 * p + k, 1), :]).astype(BF16)
            parts.append(jnp.dot(weights, xp, preferred_element_type=F32))
        rexp[:, cols] = jnp.where(carries, jnp.exp(rate_cols), 0.0)
        y[:, cols] = skip[:, cols] * xp.astype(F32) + jnp.where(first, parts[0], parts[1])

    def in_group(c, m, carried, cols):
        carried = jnp.where((q == 0) & (m == shift), 0.0, carried)
        later = pexp[pl.ds(m, 1), c * width + cols.start : c * width + cols.stop] * carried
        return carried, later + ra[c, m, :, cols].astype(F32)

    def part(b):
        return slice(b * part_width, (b + 1) * part_width)

    def group_total(c):
        if c == 0:
            pl.semaphore_wait(round_sem.at[1], 2)
            start(gpas_copy, nq)
        wait(a_copy, ni, c)
        for b in range(nb):
            total = jnp.zeros((rows_a, part_width), F32)
            for m in range(ni):
                total = in_group(c, m, total, part(b))[1]
            gs[c, b * nr : (b + 1) * nr] = total.astype(BF16).reshape(nr, rows_b, part_width)
        start(b_copy, nq, c)
        rb[c, pl.ds(q, 1)] = gs[c, pl.ds(q, 1)]

    def over_groups(c):
        if c == 0:
            wait(gpas_copy, nq)
            every = expand_rows(gpas_r[:, 0, :])
            for n in range(nc):
                for b in range(nb):

                    @pl.when(q // nr == b)
                    def _():
                        gexp[n] = every[:, n * width + b * part_width : n * width + (b + 1) * part_width]

        wait(b_copy, nq, c)

        def pass_on(k, carried):
            kb[c, k] = carried.astype(BF16)
            return gexp[c, pl.ds(k, 1), :] * carried + rb[c, k].astype(F32)

        kb[c, 0] = lax.fori_loop(0, nq, pass_on, jnp.zeros((rows_b, part_width), F32)).astype(BF16)
        start(k_copy, nq, c)
        kr[c, pl.ds(q, 1)] = kb[c, pl.ds(q, 1)]

    def to_devices(c):
        wait(k_copy, nq, c)
        for b in range(nb):
            carried = kr[c, b * nr : (b + 1) * nr].astype(F32).reshape(rows_a, part_width)
            for m in range(ni):
                entering, carried = in_group(c, m, carried, part(b))
                eb[c, m, :, part(b)] = entering.astype(BF16)
        start(e_copy, ni, c)
        ent[c, pl.ds(i, 1)] = eb[c, pl.ds(i, 1)]

    def finish(c):
        wait(e_copy, ni, c)
        cols = slice(c * width, (c + 1) * width)
        read = jnp.dot(csel[...], ent[c].reshape(state, width), preferred_element_type=F32)
        out[:, cols] = (y[:, cols] + read * rexp[:, cols]).astype(BF16)

    for stage in (group_total, over_groups, to_devices, finish):
        for c in range(nc):
            stage(c)


def on_device(nx, ni, nr, nc, *args):
    (ssm_input, bc_input, conv_taps, conv_bias, bc_taps, bc_bias, step_input, step_bias, decay_log, skip_gain,
     request_offset) = args
    tok, chans = ssm_input.shape
    state = bc_input.shape[1]
    heads = step_input.shape[0]
    nq = lax.axis_size("seq") // ni
    width, rows_a = chans // nc, state // ni
    rows_b, part_width = rows_a // nr, width // (nq // nr)
    anywhere = pl.BlockSpec(memory_space=pl.ANY)
    operands = (
        ssm_input, bc_input, conv_taps, conv_bias[None], bc_taps, bc_bias[None], step_input, step_bias[None],
        decay_log[None], skip_gain[None], request_offset[None],
    )
    vmem, dma = pltpu.VMEM, pltpu.SemaphoreType.DMA
    scratch = [
        *[vmem(a.shape, a.dtype) for a in operands],
        vmem((tok + 8, chans), F32),
        vmem((tok + 8, state), F32),
        vmem((tok, chans), BF16),
        vmem((tok, LANES), F32),
        vmem((tok, chans), F32),
        vmem((tok, chans), BF16),
        vmem((tok, chans), F32),
        vmem((heads, tok), F32),
        vmem((heads, tok), F32),
        vmem((1, chans), F32),
        vmem((16, chans), BF16),
        vmem((16, state), BF16),
        vmem((tok, state), BF16),
        vmem((tok, state), BF16),
        vmem((tok, state), BF16),
        vmem((tok, state), BF16),
        vmem((tok, tok), F32),
        vmem((tok, chans), F32),
        vmem((nc, ni, rows_a, width), BF16),
        vmem((nc, ni, rows_a, width), BF16),
        vmem((nc, nq, rows_b, part_width), BF16),
        vmem((nc, nq, rows_b, part_width), BF16),
        vmem((nc, nq, rows_b, part_width), BF16),
        vmem((nc, nq, rows_b, part_width), BF16),
        vmem((nc, ni, rows_a, width), BF16),
        vmem((nc, ni, rows_a, width), BF16),
        vmem((8, LANES), F32),
        vmem((8, 8, LANES), F32),
        vmem((8, LANES), F32),
        vmem((nq, 8, LANES), F32),
        vmem((8, chans), F32),
        vmem((nc, nq, part_width), F32),
        dma((len(operands),)),
        *[dma((nc, n)) for n in (ni, nq, nq, ni) for _ in range(2)],
        *[dma((n,)) for n in (ni, nq, 3) for _ in range(2)],
        pltpu.SemaphoreType.REGULAR((2,)),
    ]
    return pl.pallas_call(
        functools.partial(kernel, nx, ni, nr, nc),
        out_shape=jax.ShapeDtypeStruct((tok, chans), BF16),
        in_specs=[anywhere] * len(operands),
        out_specs=pl.BlockSpec(memory_space=pltpu.VMEM),
        scratch_shapes=scratch,
        compiler_params=pltpu.CompilerParams(
            collective_id=0, has_side_effects=True, vmem_limit_bytes=56 << 20
        ),
    )(*operands)


def solution(mesh, nx=4, ni=4, nr=4, nc=2):
    return jax.shard_map(
        functools.partial(on_device, nx, ni, nr, nc),
        mesh=mesh,
        in_specs=(
            P("seq", "head"),
            P("seq", "head"),
            P(None, "head"),
            P("head"),
            P(None, "head"),
            P("head"),
            P("head", "seq"),
            P("head"),
            P("head"),
            P("head"),
            P("seq"),
        ),
        out_specs=P("seq", "head"),
        check_vma=False,
    )
```

```python
import functools

import jax
import jax.numpy as jnp
from jax import lax
from jax.experimental import pallas as pl
from jax.experimental.pallas import tpu as pltpu
from jax.sharding import PartitionSpec as P

HEADDIM = 64
LANES = 128
MESH = pl.DeviceIdType.MESH
F32 = jnp.float32
BF16 = jnp.bfloat16


def split3(value):
    high = value.astype(BF16)
    rest = value - high.astype(F32)
    mid = rest.astype(BF16)
    low = (rest - mid.astype(F32)).astype(BF16)
    return high, mid, low


def iota(shape, axis):
    return lax.broadcasted_iota(jnp.int32, shape, axis)


def silu(v):
    return v / (1.0 + jnp.exp(-v))


def kernel(
    nx, ni, nr, nc,
    xin, bcin_h, taps_h, bias_h, bct_h, bcb_h, step_h, sbias_h, dlog_h, sgain_h, off_h,
    out,
    xv, bcin, taps, bias, bct, bcb, step, sbias, dlog, sgain, off,
    xf, xfb, xc, offb, sexp, xs, rexp, rate, td, skip, xhalo, bchalo, bown, bother, bsel, csel,
    smask, y, st, ra, gs, rb, kb, kr, eb, ent, pas_s, pas_r, gpas_s, gpas_r, pexp, gexp,
    ins, a_s, a_r, b_s, b_r, k_s, k_r, e_s, e_r, q_s, q_r, p_s, p_r, h_s, h_r, round_sem,
):
    tok, chans = xv.shape
    state = bcin.shape[1]
    heads = step.shape[0]
    width = chans // nc
    count = lax.axis_size("seq")
    nq = count // ni
    nb = nq // nr
    ng = nq // nx
    rows_a, rows_b, part_width = state // ni, state // ni // nr, width // nb
    s = lax.axis_index("seq")
    head = lax.axis_index("head")
    odd = lax.rem(head, 2)
    partner = head + 1 - 2 * odd
    nxt = lax.rem(s + 1, count)
    prv = lax.rem(s + count - 1, count)
    shift = (1 - odd) * (ni // 2)
    place = lax.rem(s + shift, count)
    q, i = place // ni, lax.rem(place, ni)

    def device(q_at, i_at):
        return (lax.rem(q_at * ni + i_at + count - shift, count), head)

    def member(d):
        return lax.rem(i + d, ni)

    def group(d):
        return lax.rem(q + d, nq)

    loads = [
        pltpu.make_async_copy(src, dst, ins.at[k])
        for k, (src, dst) in enumerate(
            (
                (off_h, off), (step_h, step), (sbias_h, sbias), (dlog_h, dlog), (bcin_h, bcin), (xin, xv),
                (taps_h, taps), (bias_h, bias), (bct_h, bct), (bcb_h, bcb), (sgain_h, sgain),
            )
        )
    ]
    for load in loads:
        load.start()

    barrier = pltpu.get_barrier_semaphore()

    def greet(device_id):
        pl.semaphore_signal(barrier, inc=1, device_id=device_id, device_id_type=MESH)

    def beside(d):
        return device(q // ng * ng + lax.rem(lax.rem(q, ng) + d, ng), i)

    greet(beside(1))
    greet(beside(ng - 1))

    @pl.loop(1, ni)
    def _(d):
        greet(device(q, member(d)))

    @pl.loop(1, nx)
    def _(d):
        greet(device(group(d * ng), i))

    greet((nxt, head))
    greet((prv, head))
    greet((s, partner))

    def tell(r):
        for d in (1, ng - 1):
            pl.semaphore_signal(round_sem.at[r], inc=1, device_id=beside(d), device_id_type=MESH)

    def remote(src, dst, send, recv, device_id):
        return pltpu.make_async_remote_copy(src, dst, send, recv, device_id=device_id, device_id_type=MESH)

    def halo_copy(which):
        src = (xin, bcin_h)[which].at[pl.ds(tok - 16, 16), :]
        return remote(src, (xhalo, bchalo)[which], h_s.at[which], h_r.at[which], (nxt, head))

    def partner_copy():
        return remote(bown, bother, h_s.at[2], h_r.at[2], (s, partner))

    def pas_copy(d):
        return remote(pas_s, pas_r.at[i], q_s.at[0], q_r.at[0], device(q, member(d)))

    def gpas_copy(d):
        return remote(gpas_s, gpas_r.at[q], p_s.at[0], p_r.at[0], device(group(d), i))

    def a_copy(c, d):
        to = member(d)
        return remote(st.at[c, to], ra.at[c, i], a_s.at[c], a_r.at[c], device(q, to))

    def b_copy(c, d):
        to = group(d)
        return remote(gs.at[c, to], rb.at[c, q], b_s.at[c], b_r.at[c], device(to, i))

    def k_copy(c, d):
        to = group(d)
        return remote(kb.at[c, to], kr.at[c, q], k_s.at[c], k_r.at[c], device(to, i))

    def e_copy(c, d):
        to = member(d)
        return remote(eb.at[c, to], ent.at[c, i], e_s.at[c], e_r.at[c], device(q, to))

    def start(copy, n, *lead):
        for d in range(1, n):
            copy(*lead, d).start()

    def arrived(ref, sem):
        pltpu.make_async_copy(ref, ref, sem).wait()

    for load in loads[:4]:
        load.wait()
    off_row = jnp.minimum(off[...], tok).astype(F32)
    eye = (iota((tok, tok), 0) == iota((tok, tok), 1)).astype(BF16)
    off_rows = jnp.broadcast_to(off_row, (LANES, tok)).astype(BF16)
    offb[...] = lax.dot_general(eye, off_rows, (((1,), (1,)), ((), ())), preferred_element_type=F32)
    off_last = off_row[:, tok - 1 : tok]

    eye_h = iota((heads, heads), 0) == iota((heads, heads), 1)

    def column(row):
        return jnp.sum(jnp.where(eye_h, jnp.broadcast_to(row, (heads, heads)), 0.0), axis=1, keepdims=True)

    time_step = jnp.log1p(jnp.exp(step[...] + column(sbias[...])))
    log_decay = -jnp.exp(column(dlog[...])) * time_step
    upper = (iota((tok, tok), 0) <= iota((tok, tok), 1)).astype(F32)
    rate_row = jnp.dot(log_decay, upper, precision=lax.Precision.HIGHEST, preferred_element_type=F32)
    rate[...] = rate_row
    td[...] = time_step
    rate_last = rate_row[:, tok - 1 : tok]
    position = iota((1, tok), 1).astype(F32)
    tail = off_last >= (tok - 1) - position
    s_row = jnp.where(tail, jnp.exp(rate_last - rate_row), 0.0) * time_step
    passing = jnp.where(off_last >= tok, jnp.exp(rate_last), 0.0)

    pick = iota((heads, LANES), 0) == iota((heads, LANES), 1)
    as_row = jnp.sum(jnp.where(pick, jnp.broadcast_to(passing, (heads, LANES)), 0.0), axis=0, keepdims=True)
    pas_s[...] = jnp.broadcast_to(as_row, (8, LANES))

    spread = (lax.rem(iota((3 * heads, chans), 0), heads) == iota((3 * heads, chans), 1) // HEADDIM).astype(BF16)

    def expand(value):
        return lax.dot_general(
            jnp.concatenate(split3(value), axis=0), spread, (((0,), (0,)), ((), ())), preferred_element_type=F32
        )

    sexp[...] = expand(s_row)
    rexp[...] = expand(rate_row)

    for load in loads[5:8]:
        load.wait()

    @pl.loop(0, chans // LANES)
    def _(n):
        cols = pl.ds(pl.multiple_of(n * LANES, LANES), LANES)
        xf[pl.ds(8, tok), cols] = xv[:, cols].astype(F32)
        acc = jnp.broadcast_to(bias[:, cols], (tok, LANES))
        for lag in range(4):
            term = taps[3 - lag : 4 - lag, cols] * xf[pl.ds(8 - lag, tok), cols]
            acc = acc + (term if lag == 0 else jnp.where(offb[...] >= lag, term, 0.0))
        xc[:, cols] = silu(acc).astype(BF16)

    pl.semaphore_wait(barrier, (ni - 1) + (nx - 1) + 5)
    halo_copy(1).start()
    halo_copy(0).start()
    tell(0)
    pas_r[pl.ds(i, 1)] = pas_s[...][None]
    start(pas_copy, ni)

    @pl.loop(0, chans // LANES)
    def _(n):
        cols = pl.ds(pl.multiple_of(n * LANES, LANES), LANES)
        xs[:, cols] = (xc[:, cols].astype(F32) * sexp[:, cols]).astype(BF16)

    loads[4].wait()
    loads[8].wait()
    loads[9].wait()
    xfb[pl.ds(8, tok), :] = bcin[...].astype(F32)
    halo_copy(1).wait()
    xfb[pl.ds(0, 8), :] = bchalo[...].astype(F32)[8:16]
    for n in range(state // LANES):
        cols = slice(n * LANES, (n + 1) * LANES)
        acc = jnp.broadcast_to(bcb[:, cols], (tok, LANES))
        for lag in range(4):
            term = bct[3 - lag : 4 - lag, cols] * xfb[pl.ds(8 - lag, tok), cols]
            acc = acc + (term if lag == 0 else jnp.where(offb[...] >= lag, term, 0.0))
        bown[:, cols] = silu(acc).astype(BF16)
    partner_copy().start()

    halo_copy(0).wait()
    xf[pl.ds(0, 8), :] = xhalo[...].astype(F32)[8:16]
    acc = jnp.broadcast_to(bias[...], (16, chans))
    off_top = offb[0:16, 0:1]
    for lag in range(4):
        term = taps[3 - lag : 4 - lag, :] * xf[pl.ds(8 - lag, 16), :]
        acc = acc + (term if lag == 0 else jnp.where(off_top >= lag, term, 0.0))
    top = silu(acc).astype(BF16)
    xc[0:16, :] = top
    xs[0:16, :] = (top.astype(F32) * sexp[0:16, :]).astype(BF16)

    partner_copy().wait()
    even = odd == 0
    bsel[...] = jnp.where(even, bown[...], bother[...])
    csel[...] = jnp.where(even, bother[...], bown[...])

    for c in range(nc):
        cols = slice(c * width, (c + 1) * width)
        block_state = lax.dot_general(bsel[...], xs[:, cols], (((0,), (0,)), ((), ())), preferred_element_type=F32)
        st[c] = block_state.astype(BF16).reshape(ni, rows_a, width)
        start(a_copy, ni, c)
        ra[c, pl.ds(i, 1)] = st[c, pl.ds(i, 1)]

    pl.semaphore_wait(round_sem.at[0], 2)
    tell(1)

    arrived(pas_r.at[pl.ds(0, ni - 1)], q_r.at[0])
    pas_all = pas_r[:, 0, :]
    product = pas_all[0:1]
    for m in range(1, ni):
        product = product * pas_all[m : m + 1]
    gpas_s[...] = jnp.broadcast_to(product, (8, LANES))
    gpas_r[pl.ds(q, 1)] = gpas_s[...][None]

    spread_l = (iota((LANES, chans), 0) == iota((LANES, chans), 1) // HEADDIM).astype(BF16)

    def expand_rows(value):
        return sum(jnp.dot(part, spread_l, preferred_element_type=F32) for part in split3(value))

    pexp[...] = expand_rows(pas_all)

    loads[10].wait()
    scores = lax.dot_general(csel[...], bsel[...], (((1,), (1,)), ((), ())), preferred_element_type=F32)
    row_i, col_j = iota((tok, tok), 0).astype(F32), iota((tok, tok), 1).astype(F32)
    linked = (col_j <= row_i) & (offb[:, 0:1] >= row_i - col_j)
    smask[...] = jnp.where(linked, scores, 0.0)
    spread_f = iota((heads, chans), 0) == iota((heads, chans), 1) // HEADDIM
    skip[...] = jnp.sum(jnp.where(spread_f, jnp.broadcast_to(column(sgain[...]), (heads, chans)), 0.0), axis=0, keepdims=True)
    first = iota((tok, LANES), 1) < HEADDIM
    carries = offb[...] >= iota((tok, LANES), 0).astype(F32) + 1.0

    @pl.loop(0, heads // 2)
    def _(p):
        cols = pl.ds(pl.multiple_of(p * LANES, LANES), LANES)
        rate_cols = rexp[:, cols]
        xp = xc[:, cols]
        parts = []
        for k in range(2):
            gap = jnp.minimum(rate_cols[:, k * HEADDIM : k * HEADDIM + 1] - rate[pl.ds(2 * p + k, 1), :], 0.0)
            weights = (smask[...] * jnp.exp(gap) * td[pl.ds(2 * p + k, 1), :]).astype(BF16)
            parts.append(jnp.dot(weights, xp, preferred_element_type=F32))
        rexp[:, cols] = jnp.where(carries, jnp.exp(rate_cols), 0.0)
        y[:, cols] = skip[:, cols] * xp.astype(F32) + jnp.where(first, parts[0], parts[1])

    def in_group(c, m, carried, cols):
        carried = jnp.where((q == 0) & (m == shift), 0.0, carried)
        later = pexp[pl.ds(m, 1), c * width + cols.start : c * width + cols.stop] * carried
        return carried, later + ra[c, m, :, cols].astype(F32)

    def part(b):
        return slice(b * part_width, (b + 1) * part_width)

    def group_total(c):
        if c == 0:
            pl.semaphore_wait(round_sem.at[1], 2)
            start(gpas_copy, nq)
        arrived(ra.at[c, pl.ds(0, ni - 1)], a_r.at[c])
        for b in range(nb):
            total = jnp.zeros((rows_a, part_width), F32)
            for m in range(ni):
                total = in_group(c, m, total, part(b))[1]
            gs[c, b * nr : (b + 1) * nr] = total.astype(BF16).reshape(nr, rows_b, part_width)
        start(b_copy, nq, c)
        rb[c, pl.ds(q, 1)] = gs[c, pl.ds(q, 1)]

    def over_groups(c):
        if c == 0:
            arrived(gpas_r.at[pl.ds(0, nq - 1)], p_r.at[0])
            every = expand_rows(gpas_r[:, 0, :])
            for n in range(nc):
                for b in range(nb):

                    @pl.when(q // nr == b)
                    def _():
                        gexp[n] = every[:, n * width + b * part_width : n * width + (b + 1) * part_width]

        arrived(rb.at[c, pl.ds(0, nq - 1)], b_r.at[c])

        def pass_on(k, carried):
            kb[c, k] = carried.astype(BF16)
            return gexp[c, pl.ds(k, 1), :] * carried + rb[c, k].astype(F32)

        kb[c, 0] = lax.fori_loop(0, nq, pass_on, jnp.zeros((rows_b, part_width), F32)).astype(BF16)
        start(k_copy, nq, c)
        kr[c, pl.ds(q, 1)] = kb[c, pl.ds(q, 1)]

    def to_devices(c):
        arrived(kr.at[c, pl.ds(0, nq - 1)], k_r.at[c])
        for b in range(nb):
            carried = kr[c, b * nr : (b + 1) * nr].astype(F32).reshape(rows_a, part_width)
            for m in range(ni):
                entering, carried = in_group(c, m, carried, part(b))
                eb[c, m, :, part(b)] = entering.astype(BF16)
        start(e_copy, ni, c)
        ent[c, pl.ds(i, 1)] = eb[c, pl.ds(i, 1)]

    def finish(c):
        arrived(ent.at[c, pl.ds(0, ni - 1)], e_r.at[c])
        cols = slice(c * width, (c + 1) * width)
        read = jnp.dot(csel[...], ent[c].reshape(state, width), preferred_element_type=F32)
        out[:, cols] = (y[:, cols] + read * rexp[:, cols]).astype(BF16)

    for stage in (group_total, over_groups, to_devices, finish):
        for c in range(nc):
            stage(c)

    arrived(pas_r.at[pl.ds(0, ni - 1)], q_s.at[0])
    arrived(gpas_r.at[pl.ds(0, nq - 1)], p_s.at[0])
    for c in range(nc):
        arrived(st.at[c, pl.ds(0, ni - 1)], a_s.at[c])
        arrived(gs.at[c, pl.ds(0, nq - 1)], b_s.at[c])
        arrived(kb.at[c, pl.ds(0, nq - 1)], k_s.at[c])
        arrived(eb.at[c, pl.ds(0, ni - 1)], e_s.at[c])


def on_device(nx, ni, nr, nc, *args):
    (ssm_input, bc_input, conv_taps, conv_bias, bc_taps, bc_bias, step_input, step_bias, decay_log, skip_gain,
     request_offset) = args
    tok, chans = ssm_input.shape
    state = bc_input.shape[1]
    heads = step_input.shape[0]
    nq = lax.axis_size("seq") // ni
    width, rows_a = chans // nc, state // ni
    rows_b, part_width = rows_a // nr, width // (nq // nr)
    anywhere = pl.BlockSpec(memory_space=pl.ANY)
    operands = (
        ssm_input, bc_input, conv_taps, conv_bias[None], bc_taps, bc_bias[None], step_input, step_bias[None],
        decay_log[None], skip_gain[None], request_offset[None],
    )
    vmem, dma = pltpu.VMEM, pltpu.SemaphoreType.DMA
    scratch = [
        *[vmem(a.shape, a.dtype) for a in operands],
        vmem((tok + 8, chans), F32),
        vmem((tok + 8, state), F32),
        vmem((tok, chans), BF16),
        vmem((tok, LANES), F32),
        vmem((tok, chans), F32),
        vmem((tok, chans), BF16),
        vmem((tok, chans), F32),
        vmem((heads, tok), F32),
        vmem((heads, tok), F32),
        vmem((1, chans), F32),
        vmem((16, chans), BF16),
        vmem((16, state), BF16),
        vmem((tok, state), BF16),
        vmem((tok, state), BF16),
        vmem((tok, state), BF16),
        vmem((tok, state), BF16),
        vmem((tok, tok), F32),
        vmem((tok, chans), F32),
        vmem((nc, ni, rows_a, width), BF16),
        vmem((nc, ni, rows_a, width), BF16),
        vmem((nc, nq, rows_b, part_width), BF16),
        vmem((nc, nq, rows_b, part_width), BF16),
        vmem((nc, nq, rows_b, part_width), BF16),
        vmem((nc, nq, rows_b, part_width), BF16),
        vmem((nc, ni, rows_a, width), BF16),
        vmem((nc, ni, rows_a, width), BF16),
        vmem((8, LANES), F32),
        vmem((8, 8, LANES), F32),
        vmem((8, LANES), F32),
        vmem((nq, 8, LANES), F32),
        vmem((8, chans), F32),
        vmem((nc, nq, part_width), F32),
        dma((len(operands),)),
        *[dma((nc,)) for _ in range(8)],
        *[dma((n,)) for n in (1, 1, 3) for _ in range(2)],
        pltpu.SemaphoreType.REGULAR((2,)),
    ]
    return pl.pallas_call(
        functools.partial(kernel, nx, ni, nr, nc),
        out_shape=jax.ShapeDtypeStruct((tok, chans), BF16),
        in_specs=[anywhere] * len(operands),
        out_specs=pl.BlockSpec(memory_space=pltpu.VMEM),
        scratch_shapes=scratch,
        compiler_params=pltpu.CompilerParams(
            collective_id=0, has_side_effects=True, vmem_limit_bytes=56 << 20
        ),
    )(*operands)


def solution(mesh, nx=4, ni=4, nr=8, nc=4):
    return jax.shard_map(
        functools.partial(on_device, nx, ni, nr, nc),
        mesh=mesh,
        in_specs=(
            P("seq", "head"),
            P("seq", "head"),
            P(None, "head"),
            P("head"),
            P(None, "head"),
            P("head"),
            P("head", "seq"),
            P("head"),
            P("head"),
            P("head"),
            P("seq"),
        ),
        out_specs=P("seq", "head"),
        check_vma=False,
    )
```

```python
import functools

import jax
import jax.numpy as jnp
from jax import lax
from jax.experimental import pallas as pl
from jax.experimental.pallas import tpu as pltpu
from jax.sharding import PartitionSpec as P

HEADDIM = 64
LANES = 128
MESH = pl.DeviceIdType.MESH
F32 = jnp.float32
BF16 = jnp.bfloat16


def split3(value):
    high = value.astype(BF16)
    rest = value - high.astype(F32)
    mid = rest.astype(BF16)
    low = (rest - mid.astype(F32)).astype(BF16)
    return high, mid, low


def iota(shape, axis):
    return lax.broadcasted_iota(jnp.int32, shape, axis)


def silu(v):
    return v / (1.0 + jnp.exp(-v))


def kernel(
    nx, ni, nr, nc,
    xin, bcin_h, taps_h, bias_h, bct_h, bcb_h, step_h, sbias_h, dlog_h, sgain_h, off_h,
    out,
    xv, bcin, taps, bias, bct, bcb, step, sbias, dlog, sgain, off,
    xf, xfb, xc, offb, sexp, xs, rexp, rate, td, skip, xhalo, bchalo, bown, bother, bsel, csel,
    smask, y, st, ra, gs, rb, kb, kr, eb, ent, pas_s, pas_r, gpas_s, gpas_r, pexp, gexp,
    ins, a_s, a_r, b_s, b_r, k_s, k_r, e_s, e_r, q_s, q_r, p_s, p_r, h_s, h_r, round_sem,
):
    tok, chans = xv.shape
    state = bcin.shape[1]
    heads = step.shape[0]
    width = chans // nc
    count = lax.axis_size("seq")
    nq = count // ni
    nb = nq // nr
    ng = nq // nx
    rows_a, rows_b, part_width = state // ni, state // ni // nr, width // nb
    s = lax.axis_index("seq")
    head = lax.axis_index("head")
    odd = lax.rem(head, 2)
    partner = head + 1 - 2 * odd
    nxt = lax.rem(s + 1, count)
    prv = lax.rem(s + count - 1, count)
    shift = (1 - odd) * (ni // 2)
    place = lax.rem(s + shift, count)
    q, i = place // ni, lax.rem(place, ni)

    def device(q_at, i_at):
        return (lax.rem(q_at * ni + i_at + count - shift, count), head)

    def member(d):
        return lax.rem(i + d, ni)

    def group(d):
        return lax.rem(q + d, nq)

    loads = [
        pltpu.make_async_copy(src, dst, ins.at[k])
        for k, (src, dst) in enumerate(
            (
                (off_h, off), (step_h, step), (sbias_h, sbias), (dlog_h, dlog), (bcin_h, bcin), (xin, xv),
                (taps_h, taps), (bias_h, bias), (bct_h, bct), (bcb_h, bcb), (sgain_h, sgain),
            )
        )
    ]
    for load in loads:
        load.start()

    barrier = pltpu.get_barrier_semaphore()

    def greet(device_id):
        pl.semaphore_signal(barrier, inc=1, device_id=device_id, device_id_type=MESH)

    def beside(d):
        return device(q // ng * ng + lax.rem(lax.rem(q, ng) + d, ng), i)

    greet(beside(1))
    greet(beside(ng - 1))

    @pl.loop(1, ni)
    def _(d):
        greet(device(q, member(d)))

    @pl.loop(1, nx)
    def _(d):
        greet(device(group(d * ng), i))

    greet((nxt, head))
    greet((prv, head))
    greet((s, partner))

    def tell(r):
        for d in (1, ng - 1):
            pl.semaphore_signal(round_sem.at[r], inc=1, device_id=beside(d), device_id_type=MESH)

    def remote(src, dst, send, recv, device_id):
        return pltpu.make_async_remote_copy(src, dst, send, recv, device_id=device_id, device_id_type=MESH)

    def halo_copy(which):
        src = (xin, bcin_h)[which].at[pl.ds(tok - 8, 8), :]
        return remote(src, (xhalo, bchalo)[which], h_s.at[which], h_r.at[which], (nxt, head))

    def partner_copy():
        return remote(bown, bother, h_s.at[2], h_r.at[2], (s, partner))

    def pas_copy(d):
        return remote(pas_s, pas_r.at[i], q_s.at[0], q_r.at[0], device(q, member(d)))

    def gpas_copy(d):
        return remote(gpas_s, gpas_r.at[q], p_s.at[0], p_r.at[0], device(group(d), i))

    def a_copy(c, d):
        to = member(d)
        return remote(st.at[c, to], ra.at[c, i], a_s.at[c], a_r.at[c], device(q, to))

    def b_copy(c, d):
        to = group(d)
        return remote(gs.at[c, to], rb.at[c, q], b_s.at[c], b_r.at[c], device(to, i))

    def k_copy(c, d):
        to = group(d)
        return remote(kb.at[c, to], kr.at[c, q], k_s.at[c], k_r.at[c], device(to, i))

    def e_copy(c, d):
        to = member(d)
        return remote(eb.at[c, to], ent.at[c, i], e_s.at[c], e_r.at[c], device(q, to))

    def start(copy, n, *lead):
        for d in range(1, n):
            copy(*lead, d).start()

    def arrived(ref, sem):
        pltpu.make_async_copy(ref, ref, sem).wait()

    for load in loads[:4]:
        load.wait()
    off_row = jnp.minimum(off[...], tok).astype(F32)
    eye = (iota((tok, tok), 0) == iota((tok, tok), 1)).astype(BF16)
    off_rows = jnp.broadcast_to(off_row, (LANES, tok)).astype(BF16)
    offb[...] = lax.dot_general(eye, off_rows, (((1,), (1,)), ((), ())), preferred_element_type=F32)
    off_last = off_row[:, tok - 1 : tok]

    eye_h = iota((heads, heads), 0) == iota((heads, heads), 1)

    def column(row):
        return jnp.sum(jnp.where(eye_h, jnp.broadcast_to(row, (heads, heads)), 0.0), axis=1, keepdims=True)

    time_step = jnp.log1p(jnp.exp(step[...] + column(sbias[...])))
    log_decay = -jnp.exp(column(dlog[...])) * time_step
    upper = (iota((tok, tok), 0) <= iota((tok, tok), 1)).astype(F32)
    rate_row = jnp.dot(log_decay, upper, precision=lax.Precision.HIGHEST, preferred_element_type=F32)
    rate[...] = rate_row
    td[...] = time_step
    rate_last = rate_row[:, tok - 1 : tok]
    position = iota((1, tok), 1).astype(F32)
    tail = off_last >= (tok - 1) - position
    s_row = jnp.where(tail, jnp.exp(rate_last - rate_row), 0.0) * time_step
    passing = jnp.where(off_last >= tok, jnp.exp(rate_last), 0.0)

    pick = iota((heads, LANES), 0) == iota((heads, LANES), 1)
    as_row = jnp.sum(jnp.where(pick, jnp.broadcast_to(passing, (heads, LANES)), 0.0), axis=0, keepdims=True)
    pas_s[...] = as_row

    spread = (lax.rem(iota((3 * heads, chans), 0), heads) == iota((3 * heads, chans), 1) // HEADDIM).astype(BF16)

    def expand(value):
        return lax.dot_general(
            jnp.concatenate(split3(value), axis=0), spread, (((0,), (0,)), ((), ())), preferred_element_type=F32
        )

    sexp[...] = expand(s_row)
    rexp[...] = expand(rate_row)

    for load in loads[5:8]:
        load.wait()

    @pl.loop(0, chans // LANES)
    def _(n):
        cols = pl.ds(pl.multiple_of(n * LANES, LANES), LANES)
        xf[pl.ds(8, tok), cols] = xv[:, cols].astype(F32)
        acc = jnp.broadcast_to(bias[:, cols], (tok, LANES))
        for lag in range(4):
            term = taps[3 - lag : 4 - lag, cols] * xf[pl.ds(8 - lag, tok), cols]
            acc = acc + (term if lag == 0 else jnp.where(offb[...] >= lag, term, 0.0))
        xc[:, cols] = silu(acc).astype(BF16)

    pl.semaphore_wait(barrier, (ni - 1) + (nx - 1) + 5)
    halo_copy(1).start()
    halo_copy(0).start()
    tell(0)
    pas_r[pl.ds(i, 1)] = pas_s[...][None]
    start(pas_copy, ni)

    @pl.loop(0, chans // LANES)
    def _(n):
        cols = pl.ds(pl.multiple_of(n * LANES, LANES), LANES)
        xs[:, cols] = (xc[:, cols].astype(F32) * sexp[:, cols]).astype(BF16)

    loads[4].wait()
    loads[8].wait()
    loads[9].wait()
    xfb[pl.ds(8, tok), :] = bcin[...].astype(F32)
    halo_copy(1).wait()
    xfb[pl.ds(0, 8), :] = bchalo[...].astype(F32)
    for n in range(state // LANES):
        cols = slice(n * LANES, (n + 1) * LANES)
        acc = jnp.broadcast_to(bcb[:, cols], (tok, LANES))
        for lag in range(4):
            term = bct[3 - lag : 4 - lag, cols] * xfb[pl.ds(8 - lag, tok), cols]
            acc = acc + (term if lag == 0 else jnp.where(offb[...] >= lag, term, 0.0))
        bown[:, cols] = silu(acc).astype(BF16)
    partner_copy().start()

    halo_copy(0).wait()
    xf[pl.ds(0, 8), :] = xhalo[...].astype(F32)
    acc = jnp.broadcast_to(bias[...], (16, chans))
    off_top = offb[0:16, 0:1]
    for lag in range(4):
        term = taps[3 - lag : 4 - lag, :] * xf[pl.ds(8 - lag, 16), :]
        acc = acc + (term if lag == 0 else jnp.where(off_top >= lag, term, 0.0))
    top = silu(acc).astype(BF16)
    xc[0:16, :] = top
    xs[0:16, :] = (top.astype(F32) * sexp[0:16, :]).astype(BF16)

    partner_copy().wait()
    even = odd == 0
    bsel[...] = jnp.where(even, bown[...], bother[...])
    csel[...] = jnp.where(even, bother[...], bown[...])

    for c in range(nc):
        cols = slice(c * width, (c + 1) * width)
        block_state = lax.dot_general(bsel[...], xs[:, cols], (((0,), (0,)), ((), ())), preferred_element_type=F32)
        st[c] = block_state.astype(BF16).reshape(ni, rows_a, width)
        start(a_copy, ni, c)
        ra[c, pl.ds(i, 1)] = st[c, pl.ds(i, 1)]

    pl.semaphore_wait(round_sem.at[0], 2)
    tell(1)

    arrived(pas_r.at[pl.ds(0, ni - 1)], q_r.at[0])
    pas_all = pas_r[:, 0, :]
    product = pas_all[0:1]
    for m in range(1, ni):
        product = product * pas_all[m : m + 1]
    gpas_s[...] = product
    gpas_r[pl.ds(q, 1)] = gpas_s[...][None]

    spread_l = (iota((LANES, chans), 0) == iota((LANES, chans), 1) // HEADDIM).astype(BF16)

    def expand_rows(value):
        return sum(jnp.dot(part, spread_l, preferred_element_type=F32) for part in split3(value))

    pexp[...] = expand_rows(pas_all)

    loads[10].wait()
    scores = lax.dot_general(csel[...], bsel[...], (((1,), (1,)), ((), ())), preferred_element_type=F32)
    row_i, col_j = iota((tok, tok), 0).astype(F32), iota((tok, tok), 1).astype(F32)
    linked = (col_j <= row_i) & (offb[:, 0:1] >= row_i - col_j)
    smask[...] = jnp.where(linked, scores, 0.0)
    spread_f = iota((heads, chans), 0) == iota((heads, chans), 1) // HEADDIM
    skip[...] = jnp.sum(jnp.where(spread_f, jnp.broadcast_to(column(sgain[...]), (heads, chans)), 0.0), axis=0, keepdims=True)
    first = iota((tok, LANES), 1) < HEADDIM
    carries = offb[...] >= iota((tok, LANES), 0).astype(F32) + 1.0

    @pl.loop(0, heads // 2)
    def _(p):
        cols = pl.ds(pl.multiple_of(p * LANES, LANES), LANES)
        rate_cols = rexp[:, cols]
        xp = xc[:, cols]
        parts = []
        for k in range(2):
            gap = jnp.minimum(rate_cols[:, k * HEADDIM : k * HEADDIM + 1] - rate[pl.ds(2 * p + k, 1), :], 0.0)
            weights = (smask[...] * jnp.exp(gap) * td[pl.ds(2 * p + k, 1), :]).astype(BF16)
            parts.append(jnp.dot(weights, xp, preferred_element_type=F32))
        rexp[:, cols] = jnp.where(carries, jnp.exp(rate_cols), 0.0)
        y[:, cols] = skip[:, cols] * xp.astype(F32) + jnp.where(first, parts[0], parts[1])

    def in_group(c, m, carried, cols):
        carried = jnp.where((q == 0) & (m == shift), 0.0, carried)
        later = pexp[pl.ds(m, 1), c * width + cols.start : c * width + cols.stop] * carried
        return carried, later + ra[c, m, :, cols].astype(F32)

    def part(b):
        return slice(b * part_width, (b + 1) * part_width)

    def group_total(c):
        if c == 0:
            pl.semaphore_wait(round_sem.at[1], 2)
            start(gpas_copy, nq)
        arrived(ra.at[c, pl.ds(0, ni - 1)], a_r.at[c])
        for b in range(nb):
            total = jnp.zeros((rows_a, part_width), F32)
            for m in range(ni):
                total = in_group(c, m, total, part(b))[1]
            gs[c, b * nr : (b + 1) * nr] = total.astype(BF16).reshape(nr, rows_b, part_width)
        start(b_copy, nq, c)
        rb[c, pl.ds(q, 1)] = gs[c, pl.ds(q, 1)]

    def over_groups(c):
        if c == 0:
            arrived(gpas_r.at[pl.ds(0, nq - 1)], p_r.at[0])
            every = expand_rows(gpas_r[:, 0, :])
            for n in range(nc):
                for b in range(nb):

                    @pl.when(q // nr == b)
                    def _():
                        gexp[n] = every[:, n * width + b * part_width : n * width + (b + 1) * part_width]

        arrived(rb.at[c, pl.ds(0, nq - 1)], b_r.at[c])

        def pass_on(k, carried):
            kb[c, k] = carried.astype(BF16)
            return gexp[c, pl.ds(k, 1), :] * carried + rb[c, k].astype(F32)

        kb[c, 0] = lax.fori_loop(0, nq, pass_on, jnp.zeros((rows_b, part_width), F32)).astype(BF16)
        start(k_copy, nq, c)
        kr[c, pl.ds(q, 1)] = kb[c, pl.ds(q, 1)]

    def to_devices(c):
        arrived(kr.at[c, pl.ds(0, nq - 1)], k_r.at[c])
        for b in range(nb):
            carried = kr[c, b * nr : (b + 1) * nr].astype(F32).reshape(rows_a, part_width)
            for m in range(ni):
                entering, carried = in_group(c, m, carried, part(b))
                eb[c, m, :, part(b)] = entering.astype(BF16)
        start(e_copy, ni, c)
        ent[c, pl.ds(i, 1)] = eb[c, pl.ds(i, 1)]

    def finish(c):
        arrived(ent.at[c, pl.ds(0, ni - 1)], e_r.at[c])
        cols = slice(c * width, (c + 1) * width)
        read = jnp.dot(csel[...], ent[c].reshape(state, width), preferred_element_type=F32)
        out[:, cols] = (y[:, cols] + read * rexp[:, cols]).astype(BF16)

    for stage in (group_total, over_groups, to_devices, finish):
        for c in range(nc):
            stage(c)

    arrived(pas_r.at[pl.ds(0, ni - 1)], q_s.at[0])
    arrived(gpas_r.at[pl.ds(0, nq - 1)], p_s.at[0])
    for c in range(nc):
        arrived(st.at[c, pl.ds(0, ni - 1)], a_s.at[c])
        arrived(gs.at[c, pl.ds(0, nq - 1)], b_s.at[c])
        arrived(kb.at[c, pl.ds(0, nq - 1)], k_s.at[c])
        arrived(eb.at[c, pl.ds(0, ni - 1)], e_s.at[c])


def on_device(nx, ni, nr, nc, *args):
    (ssm_input, bc_input, conv_taps, conv_bias, bc_taps, bc_bias, step_input, step_bias, decay_log, skip_gain,
     request_offset) = args
    tok, chans = ssm_input.shape
    state = bc_input.shape[1]
    heads = step_input.shape[0]
    nq = lax.axis_size("seq") // ni
    width, rows_a = chans // nc, state // ni
    rows_b, part_width = rows_a // nr, width // (nq // nr)
    anywhere = pl.BlockSpec(memory_space=pl.ANY)
    operands = (
        ssm_input, bc_input, conv_taps, conv_bias[None], bc_taps, bc_bias[None], step_input, step_bias[None],
        decay_log[None], skip_gain[None], request_offset[None],
    )
    vmem, dma = pltpu.VMEM, pltpu.SemaphoreType.DMA
    scratch = [
        *[vmem(a.shape, a.dtype) for a in operands],
        vmem((tok + 8, chans), F32),
        vmem((tok + 8, state), F32),
        vmem((tok, chans), BF16),
        vmem((tok, LANES), F32),
        vmem((tok, chans), F32),
        vmem((tok, chans), BF16),
        vmem((tok, chans), F32),
        vmem((heads, tok), F32),
        vmem((heads, tok), F32),
        vmem((1, chans), F32),
        vmem((8, chans), BF16),
        vmem((8, state), BF16),
        vmem((tok, state), BF16),
        vmem((tok, state), BF16),
        vmem((tok, state), BF16),
        vmem((tok, state), BF16),
        vmem((tok, tok), F32),
        vmem((tok, chans), F32),
        vmem((nc, ni, rows_a, width), BF16),
        vmem((nc, ni, rows_a, width), BF16),
        vmem((nc, nq, rows_b, part_width), BF16),
        vmem((nc, nq, rows_b, part_width), BF16),
        vmem((nc, nq, rows_b, part_width), BF16),
        vmem((nc, nq, rows_b, part_width), BF16),
        vmem((nc, ni, rows_a, width), BF16),
        vmem((nc, ni, rows_a, width), BF16),
        vmem((1, LANES), F32),
        vmem((8, 1, LANES), F32),
        vmem((1, LANES), F32),
        vmem((nq, 1, LANES), F32),
        vmem((8, chans), F32),
        vmem((nc, nq, part_width), F32),
        dma((len(operands),)),
        *[dma((nc,)) for _ in range(8)],
        *[dma((n,)) for n in (1, 1, 3) for _ in range(2)],
        pltpu.SemaphoreType.REGULAR((2,)),
    ]
    return pl.pallas_call(
        functools.partial(kernel, nx, ni, nr, nc),
        out_shape=jax.ShapeDtypeStruct((tok, chans), BF16),
        in_specs=[anywhere] * len(operands),
        out_specs=pl.BlockSpec(memory_space=pltpu.VMEM),
        scratch_shapes=scratch,
        compiler_params=pltpu.CompilerParams(
            collective_id=0, has_side_effects=True, vmem_limit_bytes=48 << 20
        ),
    )(*[pltpu.with_memory_space_constraint(a, pltpu.HBM) for a in operands])


def solution(mesh, nx=4, ni=4, nr=8, nc=4):
    return jax.shard_map(
        functools.partial(on_device, nx, ni, nr, nc),
        mesh=mesh,
        in_specs=(
            P("seq", "head"),
            P("seq", "head"),
            P(None, "head"),
            P("head"),
            P(None, "head"),
            P("head"),
            P("head", "seq"),
            P("head"),
            P("head"),
            P("head"),
            P("seq"),
        ),
        out_specs=P("seq", "head"),
        check_vma=False,
    )
```

```python
import functools

import jax
import jax.numpy as jnp
from jax import lax
from jax.experimental import pallas as pl
from jax.experimental.pallas import tpu as pltpu
from jax.sharding import PartitionSpec as P

HEADDIM = 64
LANES = 128
MESH = pl.DeviceIdType.MESH
F32 = jnp.float32
BF16 = jnp.bfloat16


def split3(value):
    high = value.astype(BF16)
    rest = value - high.astype(F32)
    mid = rest.astype(BF16)
    low = (rest - mid.astype(F32)).astype(BF16)
    return high, mid, low


def iota(shape, axis):
    return lax.broadcasted_iota(jnp.int32, shape, axis)


def silu(v):
    return v / (1.0 + jnp.exp(-v))


def kernel(
    nx, ni, nr, nc,
    xin, bcin_h, taps_h, bias_h, bct_h, bcb_h, step_h, sbias_h, dlog_h, sgain_h, off_h,
    out,
    xv, bcin, taps, bias, bct, bcb, step, sbias, dlog, sgain, off,
    xf, xfb, xc, offb, sexp, xs, rexp, rate, td, skip, xhalo, bchalo, bown, bother, bsel, csel,
    smask, y, st, ra, gs, rb, kb, kr, eb, ent, pas_s, pas_r, gpas_s, gpas_r, pexp, gexp,
    ins, a_s, a_r, b_s, b_r, k_s, k_r, e_s, e_r, q_s, q_r, p_s, p_r, h_s, h_r, round_sem,
):
    tok, chans = xv.shape
    state = bcin.shape[1]
    heads = step.shape[0]
    width = chans // nc
    count = lax.axis_size("seq")
    nq = count // ni
    nb = nq // nr
    ng = nq // nx
    rows_a, rows_b, part_width = state // ni, state // ni // nr, width // nb
    s = lax.axis_index("seq")
    head = lax.axis_index("head")
    odd = lax.rem(head, 2)
    partner = head + 1 - 2 * odd
    nxt = lax.rem(s + 1, count)
    prv = lax.rem(s + count - 1, count)
    shift = (1 - odd) * (ni // 2)
    place = lax.rem(s + shift, count)
    q, i = place // ni, lax.rem(place, ni)

    def device(q_at, i_at):
        return (lax.rem(q_at * ni + i_at + count - shift, count), head)

    def member(d):
        return lax.rem(i + d, ni)

    def group(d):
        return lax.rem(q + d, nq)

    loads = [
        pltpu.make_async_copy(src, dst, ins.at[k])
        for k, (src, dst) in enumerate(
            (
                (off_h, off), (step_h, step), (sbias_h, sbias), (dlog_h, dlog), (bcin_h, bcin), (xin, xv),
                (taps_h, taps), (bias_h, bias), (bct_h, bct), (bcb_h, bcb), (sgain_h, sgain),
            )
        )
    ]
    for load in loads:
        load.start()

    barrier = pltpu.get_barrier_semaphore()

    def greet(device_id):
        pl.semaphore_signal(barrier, inc=1, device_id=device_id, device_id_type=MESH)

    def beside(d):
        return device(q // ng * ng + lax.rem(lax.rem(q, ng) + d, ng), i)

    greet(beside(1))
    greet(beside(ng - 1))

    @pl.loop(1, ni)
    def _(d):
        greet(device(q, member(d)))

    @pl.loop(1, nx)
    def _(d):
        greet(device(group(d * ng), i))

    greet((nxt, head))
    greet((prv, head))
    greet((s, partner))

    def tell(r):
        for d in (1, ng - 1):
            pl.semaphore_signal(round_sem.at[r], inc=1, device_id=beside(d), device_id_type=MESH)

    def remote(src, dst, send, recv, device_id):
        return pltpu.make_async_remote_copy(src, dst, send, recv, device_id=device_id, device_id_type=MESH)

    def halo_copy(which):
        src = (xin, bcin_h)[which].at[pl.ds(tok - 8, 8), :]
        return remote(src, (xhalo, bchalo)[which], h_s.at[which], h_r.at[which], (nxt, head))

    def partner_copy(which):
        at = (pl.ds(0, 16), pl.ds(16, tok - 16))[which]
        return remote(bown.at[at, :], bother.at[at, :], h_s.at[2 + which], h_r.at[2 + which], (s, partner))

    def pas_copy(d):
        return remote(pas_s, pas_r.at[i], q_s.at[0], q_r.at[0], device(q, member(d)))

    def gpas_copy(d):
        return remote(gpas_s, gpas_r.at[q], p_s.at[0], p_r.at[0], device(group(d), i))

    def a_copy(c, d):
        to = member(d)
        return remote(st.at[c, to], ra.at[c, i], a_s.at[c], a_r.at[c], device(q, to))

    def b_copy(c, d):
        to = group(d)
        return remote(gs.at[c, to], rb.at[c, q], b_s.at[c], b_r.at[c], device(to, i))

    def k_copy(c, d):
        to = group(d)
        return remote(kb.at[c, to], kr.at[c, q], k_s.at[c], k_r.at[c], device(to, i))

    def e_copy(c, d):
        to = member(d)
        return remote(eb.at[c, to], ent.at[c, i], e_s.at[c], e_r.at[c], device(q, to))

    def start(copy, n, *lead):
        for d in range(1, n):
            copy(*lead, d).start()

    def arrived(ref, sem):
        pltpu.make_async_copy(ref, ref, sem).wait()

    for load in loads[:4]:
        load.wait()
    off_row = jnp.minimum(off[...], tok).astype(F32)
    eye = (iota((tok, tok), 0) == iota((tok, tok), 1)).astype(BF16)
    off_rows = jnp.broadcast_to(off_row, (LANES, tok)).astype(BF16)
    offb[...] = lax.dot_general(eye, off_rows, (((1,), (1,)), ((), ())), preferred_element_type=F32)
    off_last = off_row[:, tok - 1 : tok]

    eye_h = iota((heads, heads), 0) == iota((heads, heads), 1)

    def column(row):
        return jnp.sum(jnp.where(eye_h, jnp.broadcast_to(row, (heads, heads)), 0.0), axis=1, keepdims=True)

    time_step = jnp.log1p(jnp.exp(step[...] + column(sbias[...])))
    log_decay = -jnp.exp(column(dlog[...])) * time_step
    upper = (iota((tok, tok), 0) <= iota((tok, tok), 1)).astype(F32)
    rate_row = jnp.dot(log_decay, upper, precision=lax.Precision.HIGHEST, preferred_element_type=F32)
    rate[...] = rate_row
    td[...] = time_step
    rate_last = rate_row[:, tok - 1 : tok]
    position = iota((1, tok), 1).astype(F32)
    tail = off_last >= (tok - 1) - position
    s_row = jnp.where(tail, jnp.exp(rate_last - rate_row), 0.0) * time_step
    passing = jnp.where(off_last >= tok, jnp.exp(rate_last), 0.0)

    pick = iota((heads, LANES), 0) == iota((heads, LANES), 1)
    as_row = jnp.sum(jnp.where(pick, jnp.broadcast_to(passing, (heads, LANES)), 0.0), axis=0, keepdims=True)
    pas_s[...] = as_row

    spread = (lax.rem(iota((3 * heads, chans), 0), heads) == iota((3 * heads, chans), 1) // HEADDIM).astype(BF16)

    def expand(value):
        return lax.dot_general(
            jnp.concatenate(split3(value), axis=0), spread, (((0,), (0,)), ((), ())), preferred_element_type=F32
        )

    for load in loads[5:8]:
        load.wait()

    @pl.loop(0, chans // LANES)
    def _(n):
        cols = pl.ds(pl.multiple_of(n * LANES, LANES), LANES)
        xf[pl.ds(8, tok), cols] = xv[:, cols].astype(F32)
        acc = jnp.broadcast_to(bias[:, cols], (tok, LANES))
        for lag in range(4):
            term = taps[3 - lag : 4 - lag, cols] * xf[pl.ds(8 - lag, tok), cols]
            acc = acc + (term if lag == 0 else jnp.where(offb[...] >= lag, term, 0.0))
        xc[:, cols] = silu(acc).astype(BF16)

    for load in (loads[4], *loads[8:10]):
        load.wait()
    xfb[pl.ds(8, tok), :] = bcin[...].astype(F32)

    def conv_bc(rows):
        for n in range(state // LANES):
            cols = slice(n * LANES, (n + 1) * LANES)
            acc = jnp.broadcast_to(bcb[:, cols], (rows, LANES))
            for lag in range(4):
                term = bct[3 - lag : 4 - lag, cols] * xfb[pl.ds(8 - lag, rows), cols]
                acc = acc + (term if lag == 0 else jnp.where(offb[0:rows] >= lag, term, 0.0))
            bown[0:rows, cols] = silu(acc).astype(BF16)

    conv_bc(tok)
    pl.semaphore_wait(barrier, (ni - 1) + (nx - 1) + 5)
    halo_copy(1).start()
    halo_copy(0).start()
    partner_copy(1).start()
    tell(0)
    pas_r[pl.ds(i, 1)] = pas_s[...][None]
    start(pas_copy, ni)

    sexp[...] = expand(s_row)
    rexp[...] = expand(rate_row)

    @pl.loop(0, chans // LANES)
    def _(n):
        cols = pl.ds(pl.multiple_of(n * LANES, LANES), LANES)
        xs[:, cols] = (xc[:, cols].astype(F32) * sexp[:, cols]).astype(BF16)

    halo_copy(1).wait()
    xfb[pl.ds(0, 8), :] = bchalo[...].astype(F32)
    conv_bc(16)
    partner_copy(0).start()

    halo_copy(0).wait()
    xf[pl.ds(0, 8), :] = xhalo[...].astype(F32)
    acc = jnp.broadcast_to(bias[...], (16, chans))
    off_top = offb[0:16, 0:1]
    for lag in range(4):
        term = taps[3 - lag : 4 - lag, :] * xf[pl.ds(8 - lag, 16), :]
        acc = acc + (term if lag == 0 else jnp.where(off_top >= lag, term, 0.0))
    top = silu(acc).astype(BF16)
    xc[0:16, :] = top
    xs[0:16, :] = (top.astype(F32) * sexp[0:16, :]).astype(BF16)

    partner_copy(0).wait()
    partner_copy(1).wait()
    even = odd == 0
    bsel[...] = jnp.where(even, bown[...], bother[...])
    csel[...] = jnp.where(even, bother[...], bown[...])

    for c in range(nc):
        cols = slice(c * width, (c + 1) * width)
        block_state = lax.dot_general(bsel[...], xs[:, cols], (((0,), (0,)), ((), ())), preferred_element_type=F32)
        st[c] = block_state.astype(BF16).reshape(ni, rows_a, width)
        start(a_copy, ni, c)
        ra[c, pl.ds(i, 1)] = st[c, pl.ds(i, 1)]

    pl.semaphore_wait(round_sem.at[0], 2)
    tell(1)

    arrived(pas_r.at[pl.ds(0, ni - 1)], q_r.at[0])
    pas_all = pas_r[:, 0, :]
    product = pas_all[0:1]
    for m in range(1, ni):
        product = product * pas_all[m : m + 1]
    gpas_s[...] = product
    gpas_r[pl.ds(q, 1)] = gpas_s[...][None]

    spread_l = (iota((LANES, chans), 0) == iota((LANES, chans), 1) // HEADDIM).astype(BF16)

    def expand_rows(value):
        return sum(jnp.dot(part, spread_l, preferred_element_type=F32) for part in split3(value))

    pexp[...] = expand_rows(pas_all)

    loads[10].wait()
    scores = lax.dot_general(csel[...], bsel[...], (((1,), (1,)), ((), ())), preferred_element_type=F32)
    row_i, col_j = iota((tok, tok), 0).astype(F32), iota((tok, tok), 1).astype(F32)
    linked = (col_j <= row_i) & (offb[:, 0:1] >= row_i - col_j)
    smask[...] = jnp.where(linked, scores, 0.0)
    spread_f = iota((heads, chans), 0) == iota((heads, chans), 1) // HEADDIM
    skip[...] = jnp.sum(jnp.where(spread_f, jnp.broadcast_to(column(sgain[...]), (heads, chans)), 0.0), axis=0, keepdims=True)
    first = iota((tok, LANES), 1) < HEADDIM
    carries = offb[...] >= iota((tok, LANES), 0).astype(F32) + 1.0

    @pl.loop(0, heads // 2)
    def _(p):
        cols = pl.ds(pl.multiple_of(p * LANES, LANES), LANES)
        rate_cols = rexp[:, cols]
        xp = xc[:, cols]
        parts = []
        for k in range(2):
            gap = jnp.minimum(rate_cols[:, k * HEADDIM : k * HEADDIM + 1] - rate[pl.ds(2 * p + k, 1), :], 0.0)
            weights = (smask[...] * jnp.exp(gap) * td[pl.ds(2 * p + k, 1), :]).astype(BF16)
            parts.append(jnp.dot(weights, xp, preferred_element_type=F32))
        rexp[:, cols] = jnp.where(carries, jnp.exp(rate_cols), 0.0)
        y[:, cols] = skip[:, cols] * xp.astype(F32) + jnp.where(first, parts[0], parts[1])

    def in_group(c, m, carried, cols):
        carried = jnp.where((q == 0) & (m == shift), 0.0, carried)
        later = pexp[pl.ds(m, 1), c * width + cols.start : c * width + cols.stop] * carried
        return carried, later + ra[c, m, :, cols].astype(F32)

    def part(b):
        return slice(b * part_width, (b + 1) * part_width)

    def group_total(c):
        if c == 0:
            pl.semaphore_wait(round_sem.at[1], 2)
            start(gpas_copy, nq)
        arrived(ra.at[c, pl.ds(0, ni - 1)], a_r.at[c])
        for b in range(nb):
            total = jnp.zeros((rows_a, part_width), F32)
            for m in range(ni):
                total = in_group(c, m, total, part(b))[1]
            gs[c, b * nr : (b + 1) * nr] = total.astype(BF16).reshape(nr, rows_b, part_width)
        start(b_copy, nq, c)
        rb[c, pl.ds(q, 1)] = gs[c, pl.ds(q, 1)]

    def over_groups(c):
        if c == 0:
            arrived(gpas_r.at[pl.ds(0, nq - 1)], p_r.at[0])
            every = expand_rows(gpas_r[:, 0, :])
            for n in range(nc):
                for b in range(nb):

                    @pl.when(q // nr == b)
                    def _():
                        gexp[n] = every[:, n * width + b * part_width : n * width + (b + 1) * part_width]

        arrived(rb.at[c, pl.ds(0, nq - 1)], b_r.at[c])

        def pass_on(k, carried):
            kb[c, k] = carried.astype(BF16)
            return gexp[c, pl.ds(k, 1), :] * carried + rb[c, k].astype(F32)

        kb[c, 0] = lax.fori_loop(0, nq, pass_on, jnp.zeros((rows_b, part_width), F32)).astype(BF16)
        start(k_copy, nq, c)
        kr[c, pl.ds(q, 1)] = kb[c, pl.ds(q, 1)]

    def to_devices(c):
        arrived(kr.at[c, pl.ds(0, nq - 1)], k_r.at[c])
        for b in range(nb):
            carried = kr[c, b * nr : (b + 1) * nr].astype(F32).reshape(rows_a, part_width)
            for m in range(ni):
                entering, carried = in_group(c, m, carried, part(b))
                eb[c, m, :, part(b)] = entering.astype(BF16)
        start(e_copy, ni, c)
        ent[c, pl.ds(i, 1)] = eb[c, pl.ds(i, 1)]

    def finish(c):
        arrived(ent.at[c, pl.ds(0, ni - 1)], e_r.at[c])
        cols = slice(c * width, (c + 1) * width)
        read = jnp.dot(csel[...], ent[c].reshape(state, width), preferred_element_type=F32)
        out[:, cols] = (y[:, cols] + read * rexp[:, cols]).astype(BF16)

    for stage in (group_total, over_groups, to_devices, finish):
        for c in range(nc):
            stage(c)

    arrived(pas_r.at[pl.ds(0, ni - 1)], q_s.at[0])
    arrived(gpas_r.at[pl.ds(0, nq - 1)], p_s.at[0])
    for c in range(nc):
        arrived(st.at[c, pl.ds(0, ni - 1)], a_s.at[c])
        arrived(gs.at[c, pl.ds(0, nq - 1)], b_s.at[c])
        arrived(kb.at[c, pl.ds(0, nq - 1)], k_s.at[c])
        arrived(eb.at[c, pl.ds(0, ni - 1)], e_s.at[c])


def on_device(nx, ni, nr, nc, *args):
    (ssm_input, bc_input, conv_taps, conv_bias, bc_taps, bc_bias, step_input, step_bias, decay_log, skip_gain,
     request_offset) = args
    tok, chans = ssm_input.shape
    state = bc_input.shape[1]
    heads = step_input.shape[0]
    nq = lax.axis_size("seq") // ni
    width, rows_a = chans // nc, state // ni
    rows_b, part_width = rows_a // nr, width // (nq // nr)
    anywhere = pl.BlockSpec(memory_space=pl.ANY)
    operands = (
        ssm_input, bc_input, conv_taps, conv_bias[None], bc_taps, bc_bias[None], step_input, step_bias[None],
        decay_log[None], skip_gain[None], request_offset[None],
    )
    vmem, dma = pltpu.VMEM, pltpu.SemaphoreType.DMA
    scratch = [
        *[vmem(a.shape, a.dtype) for a in operands],
        vmem((tok + 8, chans), F32),
        vmem((tok + 8, state), F32),
        vmem((tok, chans), BF16),
        vmem((tok, LANES), F32),
        vmem((tok, chans), F32),
        vmem((tok, chans), BF16),
        vmem((tok, chans), F32),
        vmem((heads, tok), F32),
        vmem((heads, tok), F32),
        vmem((1, chans), F32),
        vmem((8, chans), BF16),
        vmem((8, state), BF16),
        vmem((tok, state), BF16),
        vmem((tok, state), BF16),
        vmem((tok, state), BF16),
        vmem((tok, state), BF16),
        vmem((tok, tok), F32),
        vmem((tok, chans), F32),
        vmem((nc, ni, rows_a, width), BF16),
        vmem((nc, ni, rows_a, width), BF16),
        vmem((nc, nq, rows_b, part_width), BF16),
        vmem((nc, nq, rows_b, part_width), BF16),
        vmem((nc, nq, rows_b, part_width), BF16),
        vmem((nc, nq, rows_b, part_width), BF16),
        vmem((nc, ni, rows_a, width), BF16),
        vmem((nc, ni, rows_a, width), BF16),
        vmem((1, LANES), F32),
        vmem((8, 1, LANES), F32),
        vmem((1, LANES), F32),
        vmem((nq, 1, LANES), F32),
        vmem((8, chans), F32),
        vmem((nc, nq, part_width), F32),
        dma((len(operands),)),
        *[dma((nc,)) for _ in range(8)],
        *[dma((n,)) for n in (1, 1, 4) for _ in range(2)],
        pltpu.SemaphoreType.REGULAR((2,)),
    ]
    return pl.pallas_call(
        functools.partial(kernel, nx, ni, nr, nc),
        out_shape=jax.ShapeDtypeStruct((tok, chans), BF16),
        in_specs=[anywhere] * len(operands),
        out_specs=pl.BlockSpec(memory_space=pltpu.VMEM),
        scratch_shapes=scratch,
        compiler_params=pltpu.CompilerParams(
            collective_id=0, has_side_effects=True, vmem_limit_bytes=48 << 20
        ),
    )(*[pltpu.with_memory_space_constraint(a, pltpu.HBM) for a in operands])


def solution(mesh, nx=4, ni=4, nr=8, nc=4):
    return jax.shard_map(
        functools.partial(on_device, nx, ni, nr, nc),
        mesh=mesh,
        in_specs=(
            P("seq", "head"),
            P("seq", "head"),
            P(None, "head"),
            P("head"),
            P(None, "head"),
            P("head"),
            P("head", "seq"),
            P("head"),
            P("head"),
            P("head"),
            P("seq"),
        ),
        out_specs=P("seq", "head"),
        check_vma=False,
    )
```

```python
import functools

import jax
import jax.numpy as jnp
from jax import lax
from jax.experimental import pallas as pl
from jax.experimental.pallas import tpu as pltpu
from jax.sharding import PartitionSpec as P

HEADDIM = 64
LANES = 128
MESH = pl.DeviceIdType.MESH
F32 = jnp.float32
BF16 = jnp.bfloat16


def split3(value):
    high = value.astype(BF16)
    rest = value - high.astype(F32)
    mid = rest.astype(BF16)
    low = (rest - mid.astype(F32)).astype(BF16)
    return high, mid, low


def iota(shape, axis):
    return lax.broadcasted_iota(jnp.int32, shape, axis)


def silu(v):
    return v / (1.0 + jnp.exp(-v))


def kernel(
    nx, ni, nr, nc,
    xin, bcin_h, taps_h, bias_h, bct_h, bcb_h, step_h, sbias_h, dlog_h, sgain_h, off_h,
    out,
    xv, bcin, taps, bias, bct, bcb, step, sbias, dlog, sgain, off,
    xf, xfb, xc, offb, sexp, xs, rexp, rate, td, skip, xhalo, bchalo, bown, bother, bsel, csel, bturned,
    smask, y, st, ra, gs, rb, kb, kr, eb, ent, pas_s, pas_r, gpas_s, gpas_r, pexp, gexp,
    ins, a_s, a_r, b_s, b_r, k_s, k_r, e_s, e_r, q_s, q_r, p_s, p_r, h_s, h_r, round_sem,
):
    tok, chans = xv.shape
    state = bcin.shape[1]
    heads = step.shape[0]
    width = chans // nc
    count = lax.axis_size("seq")
    nq = count // ni
    nb = nq // nr
    ng = nq // nx
    rows_a, rows_b, part_width = state // ni, state // ni // nr, width // nb
    s = lax.axis_index("seq")
    head = lax.axis_index("head")
    odd = lax.rem(head, 2)
    partner = head + 1 - 2 * odd
    nxt = lax.rem(s + 1, count)
    prv = lax.rem(s + count - 1, count)
    shift = (1 - odd) * (ni // 2)
    place = lax.rem(s + shift, count)
    q, i = place // ni, lax.rem(place, ni)

    def device(q_at, i_at):
        return (lax.rem(q_at * ni + i_at + count - shift, count), head)

    def member(d):
        return lax.rem(i + d, ni)

    def group(d):
        return lax.rem(q + d, nq)

    loads = [
        pltpu.make_async_copy(src, dst, ins.at[k])
        for k, (src, dst) in enumerate(
            (
                (off_h, off), (step_h, step), (sbias_h, sbias), (dlog_h, dlog), (bcin_h, bcin), (xin, xv),
                (taps_h, taps), (bias_h, bias), (bct_h, bct), (bcb_h, bcb), (sgain_h, sgain),
            )
        )
    ]
    for load in loads:
        load.start()

    barrier = pltpu.get_barrier_semaphore()

    def greet(device_id):
        pl.semaphore_signal(barrier, inc=1, device_id=device_id, device_id_type=MESH)

    def beside(d):
        return device(q // ng * ng + lax.rem(lax.rem(q, ng) + d, ng), i)

    greet(beside(1))
    greet(beside(ng - 1))

    @pl.loop(1, ni)
    def _(d):
        greet(device(q, member(d)))

    @pl.loop(1, nx)
    def _(d):
        greet(device(group(d * ng), i))

    greet((nxt, head))
    greet((prv, head))
    greet((s, partner))

    def tell(r):
        for d in (1, ng - 1):
            pl.semaphore_signal(round_sem.at[r], inc=1, device_id=beside(d), device_id_type=MESH)

    def remote(src, dst, send, recv, device_id):
        return pltpu.make_async_remote_copy(src, dst, send, recv, device_id=device_id, device_id_type=MESH)

    def halo_copy(which):
        src = (xin, bcin_h)[which].at[pl.ds(tok - 8, 8), :]
        return remote(src, (xhalo, bchalo)[which], h_s.at[which], h_r.at[which], (nxt, head))

    def partner_copy(which):
        at = (pl.ds(0, 16), pl.ds(16, tok - 16))[which]
        return remote(bown.at[at, :], bother.at[at, :], h_s.at[2 + which], h_r.at[2 + which], (s, partner))

    def pas_copy(d):
        return remote(pas_s, pas_r.at[i], q_s.at[0], q_r.at[0], device(q, member(d)))

    def gpas_copy(d):
        return remote(gpas_s, gpas_r.at[q], p_s.at[0], p_r.at[0], device(group(d), i))

    def a_copy(c, d):
        to = member(d)
        return remote(st.at[c, to], ra.at[c, i], a_s.at[c], a_r.at[c], device(q, to))

    def b_copy(c, d):
        to = group(d)
        return remote(gs.at[c, to], rb.at[c, q], b_s.at[c], b_r.at[c], device(to, i))

    def k_copy(c, d):
        to = group(d)
        return remote(kb.at[c, to], kr.at[c, q], k_s.at[c], k_r.at[c], device(to, i))

    def e_copy(c, d):
        to = member(d)
        return remote(eb.at[c, to], ent.at[c, i], e_s.at[c], e_r.at[c], device(q, to))

    def start(copy, n, *lead):
        for d in range(1, n):
            copy(*lead, d).start()

    def arrived(ref, sem):
        pltpu.make_async_copy(ref, ref, sem).wait()

    for load in loads[:4]:
        load.wait()
    off_row = jnp.minimum(off[...], tok).astype(F32)
    eye = (iota((tok, tok), 0) == iota((tok, tok), 1)).astype(BF16)
    off_rows = jnp.broadcast_to(off_row, (LANES, tok)).astype(BF16)
    offb[...] = lax.dot_general(eye, off_rows, (((1,), (1,)), ((), ())), preferred_element_type=F32)
    off_last = off_row[:, tok - 1 : tok]

    eye_h = iota((heads, heads), 0) == iota((heads, heads), 1)

    def column(row):
        return jnp.sum(jnp.where(eye_h, jnp.broadcast_to(row, (heads, heads)), 0.0), axis=1, keepdims=True)

    time_step = jnp.log1p(jnp.exp(step[...] + column(sbias[...])))
    log_decay = -jnp.exp(column(dlog[...])) * time_step
    upper = (iota((tok, tok), 0) <= iota((tok, tok), 1)).astype(F32)
    rate_row = jnp.dot(log_decay, upper, precision=lax.Precision.HIGHEST, preferred_element_type=F32)
    rate[...] = rate_row
    td[...] = time_step
    rate_last = rate_row[:, tok - 1 : tok]
    position = iota((1, tok), 1).astype(F32)
    tail = off_last >= (tok - 1) - position
    s_row = jnp.where(tail, jnp.exp(rate_last - rate_row), 0.0) * time_step
    passing = jnp.where(off_last >= tok, jnp.exp(rate_last), 0.0)

    pick = iota((heads, LANES), 0) == iota((heads, LANES), 1)
    as_row = jnp.sum(jnp.where(pick, jnp.broadcast_to(passing, (heads, LANES)), 0.0), axis=0, keepdims=True)
    pas_s[...] = as_row

    spread = (lax.rem(iota((3 * heads, chans), 0), heads) == iota((3 * heads, chans), 1) // HEADDIM).astype(BF16)

    def expand(value):
        return lax.dot_general(
            jnp.concatenate(split3(value), axis=0), spread, (((0,), (0,)), ((), ())), preferred_element_type=F32
        )

    for load in loads[5:8]:
        load.wait()

    @pl.loop(0, chans // LANES)
    def _(n):
        cols = pl.ds(pl.multiple_of(n * LANES, LANES), LANES)
        xf[pl.ds(8, tok), cols] = xv[:, cols].astype(F32)
        acc = jnp.broadcast_to(bias[:, cols], (tok, LANES))
        for lag in range(4):
            term = taps[3 - lag : 4 - lag, cols] * xf[pl.ds(8 - lag, tok), cols]
            acc = acc + (term if lag == 0 else jnp.where(offb[...] >= lag, term, 0.0))
        xc[:, cols] = silu(acc).astype(BF16)

    for load in (loads[4], *loads[8:10]):
        load.wait()
    xfb[pl.ds(8, tok), :] = bcin[...].astype(F32)

    def conv_bc(rows):
        for n in range(state // LANES):
            cols = slice(n * LANES, (n + 1) * LANES)
            acc = jnp.broadcast_to(bcb[:, cols], (rows, LANES))
            for lag in range(4):
                term = bct[3 - lag : 4 - lag, cols] * xfb[pl.ds(8 - lag, rows), cols]
                acc = acc + (term if lag == 0 else jnp.where(offb[0:rows] >= lag, term, 0.0))
            bown[0:rows, cols] = silu(acc).astype(BF16)

    conv_bc(tok)
    pl.semaphore_wait(barrier, (ni - 1) + (nx - 1) + 5)
    halo_copy(1).start()
    halo_copy(0).start()
    partner_copy(1).start()
    tell(0)
    pas_r[pl.ds(i, 1)] = pas_s[...][None]
    start(pas_copy, ni)

    sexp[...] = expand(s_row)
    rexp[...] = expand(rate_row)

    @pl.loop(0, chans // LANES)
    def _(n):
        cols = pl.ds(pl.multiple_of(n * LANES, LANES), LANES)
        xs[:, cols] = (xc[:, cols].astype(F32) * sexp[:, cols]).astype(BF16)

    halo_copy(1).wait()
    xfb[pl.ds(0, 8), :] = bchalo[...].astype(F32)
    conv_bc(16)
    partner_copy(0).start()

    halo_copy(0).wait()
    xf[pl.ds(0, 8), :] = xhalo[...].astype(F32)
    acc = jnp.broadcast_to(bias[...], (16, chans))
    off_top = offb[0:16, 0:1]
    for lag in range(4):
        term = taps[3 - lag : 4 - lag, :] * xf[pl.ds(8 - lag, 16), :]
        acc = acc + (term if lag == 0 else jnp.where(off_top >= lag, term, 0.0))
    top = silu(acc).astype(BF16)
    xc[0:16, :] = top
    xs[0:16, :] = (top.astype(F32) * sexp[0:16, :]).astype(BF16)

    partner_copy(0).wait()
    partner_copy(1).wait()
    even = odd == 0
    b_rows = jnp.where(even, bown[...], bother[...])
    bsel[...] = b_rows
    bturned[...] = b_rows.T
    csel[...] = jnp.where(even, bother[...], bown[...])

    for c in range(nc):
        cols = slice(c * width, (c + 1) * width)
        block_state = jnp.dot(bturned[...], xs[:, cols], preferred_element_type=F32)
        st[c] = block_state.astype(BF16).reshape(ni, rows_a, width)
        start(a_copy, ni, c)
        ra[c, pl.ds(i, 1)] = st[c, pl.ds(i, 1)]

    pl.semaphore_wait(round_sem.at[0], 2)
    tell(1)

    arrived(pas_r.at[pl.ds(0, ni - 1)], q_r.at[0])
    pas_all = pas_r[:, 0, :]
    product = pas_all[0:1]
    for m in range(1, ni):
        product = product * pas_all[m : m + 1]
    gpas_s[...] = product
    gpas_r[pl.ds(q, 1)] = gpas_s[...][None]

    spread_l = (iota((LANES, chans), 0) == iota((LANES, chans), 1) // HEADDIM).astype(BF16)

    def expand_rows(value):
        return sum(jnp.dot(part, spread_l, preferred_element_type=F32) for part in split3(value))

    pexp[...] = expand_rows(pas_all)

    loads[10].wait()
    scores = lax.dot_general(csel[...], bsel[...], (((1,), (1,)), ((), ())), preferred_element_type=F32)
    row_i, col_j = iota((tok, tok), 0).astype(F32), iota((tok, tok), 1).astype(F32)
    linked = (col_j <= row_i) & (offb[:, 0:1] >= row_i - col_j)
    smask[...] = jnp.where(linked, scores, 0.0)
    spread_f = iota((heads, chans), 0) == iota((heads, chans), 1) // HEADDIM
    skip[...] = jnp.sum(jnp.where(spread_f, jnp.broadcast_to(column(sgain[...]), (heads, chans)), 0.0), axis=0, keepdims=True)
    first = iota((tok, LANES), 1) < HEADDIM
    carries = offb[...] >= iota((tok, LANES), 0).astype(F32) + 1.0

    @pl.loop(0, heads // 2)
    def _(p):
        cols = pl.ds(pl.multiple_of(p * LANES, LANES), LANES)
        rate_cols = rexp[:, cols]
        xp = xc[:, cols]
        parts = []
        for k in range(2):
            gap = jnp.minimum(rate_cols[:, k * HEADDIM : k * HEADDIM + 1] - rate[pl.ds(2 * p + k, 1), :], 0.0)
            weights = (smask[...] * jnp.exp(gap) * td[pl.ds(2 * p + k, 1), :]).astype(BF16)
            parts.append(jnp.dot(weights, xp, preferred_element_type=F32))
        rexp[:, cols] = jnp.where(carries, jnp.exp(rate_cols), 0.0)
        y[:, cols] = skip[:, cols] * xp.astype(F32) + jnp.where(first, parts[0], parts[1])

    def in_group(c, m, carried, cols):
        carried = jnp.where((q == 0) & (m == shift), 0.0, carried)
        later = pexp[pl.ds(m, 1), c * width + cols.start : c * width + cols.stop] * carried
        return carried, later + ra[c, m, :, cols].astype(F32)

    def part(b):
        return slice(b * part_width, (b + 1) * part_width)

    def group_total(c):
        if c == 0:
            pl.semaphore_wait(round_sem.at[1], 2)
            start(gpas_copy, nq)
        arrived(ra.at[c, pl.ds(0, ni - 1)], a_r.at[c])
        for b in range(nb):
            total = jnp.zeros((rows_a, part_width), F32)
            for m in range(ni):
                total = in_group(c, m, total, part(b))[1]
            gs[c, b * nr : (b + 1) * nr] = total.astype(BF16).reshape(nr, rows_b, part_width)
        start(b_copy, nq, c)
        rb[c, pl.ds(q, 1)] = gs[c, pl.ds(q, 1)]

    def over_groups(c):
        if c == 0:
            arrived(gpas_r.at[pl.ds(0, nq - 1)], p_r.at[0])
            every = expand_rows(gpas_r[:, 0, :])
            for n in range(nc):
                for b in range(nb):

                    @pl.when(q // nr == b)
                    def _():
                        gexp[n] = every[:, n * width + b * part_width : n * width + (b + 1) * part_width]

        arrived(rb.at[c, pl.ds(0, nq - 1)], b_r.at[c])

        def pass_on(k, carried):
            kb[c, k] = carried.astype(BF16)
            return gexp[c, pl.ds(k, 1), :] * carried + rb[c, k].astype(F32)

        kb[c, 0] = lax.fori_loop(0, nq, pass_on, jnp.zeros((rows_b, part_width), F32)).astype(BF16)
        start(k_copy, nq, c)
        kr[c, pl.ds(q, 1)] = kb[c, pl.ds(q, 1)]

    def to_devices(c):
        arrived(kr.at[c, pl.ds(0, nq - 1)], k_r.at[c])
        for b in range(nb):
            carried = kr[c, b * nr : (b + 1) * nr].astype(F32).reshape(rows_a, part_width)
            for m in range(ni):
                entering, carried = in_group(c, m, carried, part(b))
                eb[c, m, :, part(b)] = entering.astype(BF16)
        start(e_copy, ni, c)
        ent[c, pl.ds(i, 1)] = eb[c, pl.ds(i, 1)]

    def finish(c):
        arrived(ent.at[c, pl.ds(0, ni - 1)], e_r.at[c])
        cols = slice(c * width, (c + 1) * width)
        read = jnp.dot(csel[...], ent[c].reshape(state, width), preferred_element_type=F32)
        out[:, cols] = (y[:, cols] + read * rexp[:, cols]).astype(BF16)

    for stage in (group_total, over_groups, to_devices, finish):
        for c in range(nc):
            stage(c)

    arrived(pas_r.at[pl.ds(0, ni - 1)], q_s.at[0])
    arrived(gpas_r.at[pl.ds(0, nq - 1)], p_s.at[0])
    for c in range(nc):
        arrived(st.at[c, pl.ds(0, ni - 1)], a_s.at[c])
        arrived(gs.at[c, pl.ds(0, nq - 1)], b_s.at[c])
        arrived(kb.at[c, pl.ds(0, nq - 1)], k_s.at[c])
        arrived(eb.at[c, pl.ds(0, ni - 1)], e_s.at[c])


def on_device(nx, ni, nr, nc, *args):
    (ssm_input, bc_input, conv_taps, conv_bias, bc_taps, bc_bias, step_input, step_bias, decay_log, skip_gain,
     request_offset) = args
    tok, chans = ssm_input.shape
    state = bc_input.shape[1]
    heads = step_input.shape[0]
    nq = lax.axis_size("seq") // ni
    width, rows_a = chans // nc, state // ni
    rows_b, part_width = rows_a // nr, width // (nq // nr)
    anywhere = pl.BlockSpec(memory_space=pl.ANY)
    operands = (
        ssm_input, bc_input, conv_taps, conv_bias[None], bc_taps, bc_bias[None], step_input, step_bias[None],
        decay_log[None], skip_gain[None], request_offset[None],
    )
    vmem, dma = pltpu.VMEM, pltpu.SemaphoreType.DMA
    scratch = [
        *[vmem(a.shape, a.dtype) for a in operands],
        vmem((tok + 8, chans), F32),
        vmem((tok + 8, state), F32),
        vmem((tok, chans), BF16),
        vmem((tok, LANES), F32),
        vmem((tok, chans), F32),
        vmem((tok, chans), BF16),
        vmem((tok, chans), F32),
        vmem((heads, tok), F32),
        vmem((heads, tok), F32),
        vmem((1, chans), F32),
        vmem((8, chans), BF16),
        vmem((8, state), BF16),
        vmem((tok, state), BF16),
        vmem((tok, state), BF16),
        vmem((tok, state), BF16),
        vmem((tok, state), BF16),
        vmem((state, tok), BF16),
        vmem((tok, tok), F32),
        vmem((tok, chans), F32),
        vmem((nc, ni, rows_a, width), BF16),
        vmem((nc, ni, rows_a, width), BF16),
        vmem((nc, nq, rows_b, part_width), BF16),
        vmem((nc, nq, rows_b, part_width), BF16),
        vmem((nc, nq, rows_b, part_width), BF16),
        vmem((nc, nq, rows_b, part_width), BF16),
        vmem((nc, ni, rows_a, width), BF16),
        vmem((nc, ni, rows_a, width), BF16),
        vmem((1, LANES), F32),
        vmem((8, 1, LANES), F32),
        vmem((1, LANES), F32),
        vmem((nq, 1, LANES), F32),
        vmem((8, chans), F32),
        vmem((nc, nq, part_width), F32),
        dma((len(operands),)),
        *[dma((nc,)) for _ in range(8)],
        *[dma((n,)) for n in (1, 1, 4) for _ in range(2)],
        pltpu.SemaphoreType.REGULAR((2,)),
    ]
    return pl.pallas_call(
        functools.partial(kernel, nx, ni, nr, nc),
        out_shape=jax.ShapeDtypeStruct((tok, chans), BF16),
        in_specs=[anywhere] * len(operands),
        out_specs=pl.BlockSpec(memory_space=pltpu.VMEM),
        scratch_shapes=scratch,
        compiler_params=pltpu.CompilerParams(
            collective_id=0, has_side_effects=True, vmem_limit_bytes=48 << 20
        ),
    )(*[pltpu.with_memory_space_constraint(a, pltpu.HBM) for a in operands])


def solution(mesh, nx=4, ni=4, nr=8, nc=4):
    return jax.shard_map(
        functools.partial(on_device, nx, ni, nr, nc),
        mesh=mesh,
        in_specs=(
            P("seq", "head"),
            P("seq", "head"),
            P(None, "head"),
            P("head"),
            P(None, "head"),
            P("head"),
            P("head", "seq"),
            P("head"),
            P("head"),
            P("head"),
            P("seq"),
        ),
        out_specs=P("seq", "head"),
        check_vma=False,
    )
```
